256 devices in a mesh: segment: 8 (over x_lo, y), lat: 16 (over z, x_hi), dp: 2 (over core).
Axes of the slice: x: 4 (x_hi: 2, x_lo: 2; x = x_hi * 2 + x_lo), y: 4, z: 8, core: 2. Of those that a mesh axis runs over, the one named last changes fastest.
Arguments:
- initial: bfloat16 [8, 192, 32, 128], P('dp', None, 'lat'), may hold values from -6 to 6
- kernel: bfloat16 [8, 192, 9, 192], P('segment'), may hold values from -0.078125 to 0.078125
- bias: float32 [8, 192], P('segment'), may hold values from -0.6 to 0.6
- cotangent: bfloat16 [2, 8, 192, 32, 128], P(None, 'dp', None, 'lat'), may hold values from -6 to 6
Outputs:
- section_out: bfloat16 [8, 8, 192, 32, 128], P('segment', 'dp', None, 'lat')
- state_adjoint: float32 [8, 8, 192, 32, 128], P('segment', 'dp', None, 'lat')
- kernel_grad: float32 [8, 192, 9, 192], P('segment')
- bias_grad: float32 [8, 192], P('segment')
The draws below stay inside these ranges and needn't reach their ends.
All inputs are finite; a program needn't handle non-finite values.
Results may differ from the reference program's by a relative error of at most 0.028.
Values may be sent and summed in bfloat16 or wider, within the bound.
A program may use at most 64 MiB of HBM per device.

```python
import math
import jax
import jax.numpy as jnp
from jax import lax

C = 192
W = 128
STEPS = 2
SECTIONS = 8
H = 32
SAMPLES = 8


def steps_of(rng, extent, split, smallest, largest):
    loudness, own = 1.0, jax.random.fold_in(rng, 6)
    for axis_at, parts in split:
        heights = jnp.exp(jax.random.uniform(jax.random.fold_in(own, axis_at), (parts,), jnp.float32, smallest / len(split), largest / len(split)))
        loudness = loudness * jnp.repeat(heights, extent[axis_at] // parts).reshape([-1 if axis == axis_at else 1 for axis in range(len(extent))])
    return loudness


def scatter_about(stream_key, dims, scale, most, cuts=(), kind=jnp.bfloat16):
    gain = steps_of(stream_key, dims, cuts, -0.22, 0.18) if cuts else 1.0
    drawn = jax.random.normal(stream_key, dims, jnp.float32) * scale * gain
    return jnp.minimum(jnp.maximum(drawn, -most), most).astype(kind)


def setup_inputs(seed: int = 0) -> dict:
    seeds = jax.random.split(jax.random.key(seed), 5)
    return {
        "initial": scatter_about(seeds[0], (SAMPLES, C, H, W), 1.0, 6.0, ((0, 2), (2, 16))),
        "kernel": scatter_about(seeds[1], (SECTIONS, C, 9, C), (36 * C) ** -0.5, 0.078125, ((0, 8),)),
        "bias": scatter_about(seeds[2], (SECTIONS, C), 0.1, 0.6, ((0, 8),), jnp.float32),
        "cotangent": scatter_about(seeds[3], (STEPS, SAMPLES, C, H, W), 1.0, 6.0, ((1, 2), (3, 16))),
    }


def silu_value(values):
    return values / (1.0 + jnp.exp(-values))

def silu_slope(values):
    sigmoid_v = 1.0 / (1.0 + jnp.exp(-values))
    return sigmoid_v * (1.0 + values * (1.0 - sigmoid_v))

def tap_columns(padded):
    band_rows = padded.shape[1] - 2
    pieces = []
    for row_tap in range(3):
        strip = padded[:, row_tap:row_tap + band_rows, :]
        for col_tap in range(3):
            pieces.append(jnp.roll(strip, 1 - col_tap, axis=2))
    stacked = jnp.stack(pieces, axis=0)
    return stacked.reshape(9 * padded.shape[0], band_rows * padded.shape[2])

def back_columns(padded):
    band_rows = padded.shape[1] - 2
    pieces = []
    for row_tap in range(3):
        strip = padded[:, 2 - row_tap:2 - row_tap + band_rows, :]
        for col_tap in range(3):
            pieces.append(jnp.roll(strip, col_tap - 1, axis=2))
    stacked = jnp.stack(pieces, axis=0)
    return stacked.reshape(9, padded.shape[0], band_rows * padded.shape[2])

def pad_rows(values):
    return jnp.pad(values, ((0, 0), (1, 1), (0, 0)))

def reference(initial, kernel, bias, cotangent):
    flat_kernel = kernel.reshape(SECTIONS, C, 9 * C)
    normalizer = 1.0 / math.sqrt(SAMPLES * H * W)
    applications = STEPS * SECTIONS

    def one_sample(inputs):
        first_state, sample_cots = inputs
        states = [first_state]
        for position in range(applications):
            section = position % SECTIONS
            current = states[-1]
            activated = silu_value(current.astype(jnp.float32)).astype(jnp.bfloat16)
            branch = jnp.dot(flat_kernel[section], tap_columns(pad_rows(activated)), preferred_element_type=jnp.float32).reshape(C, H, W)
            updated = current.astype(jnp.float32) + branch + bias[section].astype(jnp.float32)[:, None, None]
            states.append(updated.astype(jnp.bfloat16))
        last_outputs = jnp.stack(states[applications - SECTIONS + 1:], axis=0)
        kernel_sum = jnp.zeros((SECTIONS, C, 9 * C), jnp.float32)
        bias_sum = jnp.zeros((SECTIONS, C), jnp.float32)
        first_adjoints = [None] * SECTIONS
        incoming = sample_cots[STEPS - 1]
        for position in reversed(range(applications)):
            section = position % SECTIONS
            current = states[position]
            activated = silu_value(current.astype(jnp.float32)).astype(jnp.bfloat16)
            columns = tap_columns(pad_rows(activated))
            gradient_rows = incoming.reshape(C, H * W)
            kernel_term = lax.dot_general(gradient_rows, columns, (((1,), (1,)), ((), ())), preferred_element_type=jnp.float32)
            kernel_sum = kernel_sum.at[section].add(kernel_term)
            bias_sum = bias_sum.at[section].add(lax.optimization_barrier(jnp.sum(incoming.astype(jnp.float32), axis=(1, 2))))
            transposed = lax.dot_general(kernel[section], back_columns(pad_rows(incoming)), (((0, 1), (1, 0)), ((), ())), preferred_element_type=jnp.float32).reshape(C, H, W)
            adjoint_here = incoming.astype(jnp.float32) + silu_slope(current.astype(jnp.float32)) * transposed
            if position >= SECTIONS and position % SECTIONS == 0:
                adjoint_here = adjoint_here + sample_cots[position // SECTIONS - 1].astype(jnp.float32)
            if position < SECTIONS:
                first_adjoints[position] = adjoint_here
            incoming = adjoint_here.astype(jnp.bfloat16)
        return (last_outputs, jnp.stack(first_adjoints, axis=0), kernel_sum, bias_sum)
    outputs, adjoints, kernel_parts, bias_parts = lax.map(one_sample, (initial, jnp.moveaxis(cotangent, 1, 0)))
    section_out = jnp.moveaxis(outputs, 1, 0)
    state_adjoint = jnp.moveaxis(adjoints, 1, 0)
    kernel_grad = (lax.optimization_barrier(jnp.sum(kernel_parts, axis=0)) * normalizer).reshape(SECTIONS, C, 9, C)
    bias_grad = lax.optimization_barrier(jnp.sum(bias_parts, axis=0)) * normalizer
    return (section_out, state_adjoint, kernel_grad, bias_grad)
```

```python
import functools
import math

import jax
import jax.numpy as jnp
from jax import lax
from jax.experimental import pallas as pl
from jax.experimental.pallas import tpu as pltpu
from jax.sharding import PartitionSpec as P

STEPS = 2
SECTIONS = 8
APPS = STEPS * SECTIONS
BF = jnp.bfloat16
F32 = jnp.float32
MESH = pl.DeviceIdType.MESH
HALO_UP, HALO_DN = 0, 1


def silu_value(values):
    return values / (1.0 + jnp.exp(-values))


def silu_slope(values):
    sigmoid_v = 1.0 / (1.0 + jnp.exp(-values))
    return sigmoid_v * (1.0 + values * (1.0 - sigmoid_v))


def units_for(lat_count, rows):
    for count in range(min(lat_count, rows // 16), 0, -1):
        if rows % (16 * count) == 0:
            return count
    return 1


def network_kernel(
    dims, x_ref, w_ref, so_ref, sa_ref, gw_ref,
    xc, wall, b2, pbuf, gbuf, sbuf, dwf, cr, cs, r2, r3st, r3, xsem, wss, wrs,
    hss, hrs, oss, ors, crs, crr, r2s, r2r, r3s, r3r, r4s, r4r, r5,
):
    C, W, nz = dims
    K3 = 3 * C
    half = K3 // 2
    part = half // 2
    lanes = w_ref.shape[1]
    nlat = 2 * nz
    nrow = 4 * nz
    nu = units_for(nlat, half)
    ur = half // nu

    seg = lax.axis_index("segment")
    lat = lax.axis_index("lat")
    core = lax.axis_index("dp")
    x_lo, y = seg // 4, lax.rem(seg, 4)
    z, x_hi = lat // 2, lax.rem(lat, 2)
    x = 2 * x_hi + x_lo
    odd = lax.rem(z, 2)
    xr = x + odd * (3 - 2 * x)
    row = 4 * z + xr
    has_up = row > 0
    has_dn = row < nrow - 1

    def at(px, py, pz, pc=core):
        return {"segment": lax.rem(px, 2) * 4 + py, "lat": pz * 2 + px // 2, "dp": pc}

    def holder(r):
        rz = r // 4
        rx = lax.rem(r, 4)
        return at(rx + lax.rem(rz, 2) * (3 - 2 * rx), y, rz)

    up_dev = holder(jnp.maximum(row - 1, 0))
    dn_dev = holder(jnp.minimum(row + 1, nrow - 1))
    other = 1 - core
    partner = {"segment": seg, "lat": lat, "dp": other}
    y_up, y_dn = lax.rem(y + 1, 4), lax.rem(y + 3, 4)
    x_up, x_dn = lax.rem(x + 1, 4), lax.rem(x + 3, 4)

    barrier = pltpu.get_barrier_semaphore()
    for d in range(1, 16):
        dx, dy = d // 4, d % 4
        pl.semaphore_signal(
            barrier, inc=1, device_id=at(lax.rem(x + dx, 4), lax.rem(y + dy, 4), z), device_id_type=MESH
        )
    for d in range(1, nz):
        for hi in range(2):
            peer = {"segment": seg, "lat": lax.rem(z + d, nz) * 2 + hi, "dp": core}
            pl.semaphore_signal(barrier, inc=1, device_id=peer, device_id_type=MESH)
    pl.semaphore_signal(barrier, inc=1, device_id=partner, device_id_type=MESH)
    pl.semaphore_wait(barrier, 15 + 2 * (nz - 1) + 1)

    def remote(src, dst, ssem, rsem, dev):
        return pltpu.make_async_remote_copy(
            src_ref=src, dst_ref=dst, send_sem=ssem, recv_sem=rsem, device_id=dev, device_id_type=MESH
        )

    swap = remote(x_ref, xc, xsem.at[0], xsem.at[1], at(3 - x, y, z))

    @pl.when(odd == 1)
    def _():
        swap.start()

    wall[seg] = w_ref[...].reshape(2, 2, part, lanes)
    sec_dn, sec_up = x_lo * 4 + y_dn, x_lo * 4 + y_up
    sec_far = x_lo * 4 + lax.rem(y + 2, 4)
    sends = []

    def go(copy):
        copy.start()
        sends.append(copy)

    def send_w(index, src, slot, dev):
        go(remote(src, src, wss.at[index], wrs.at[slot], dev))

    dev_yu, dev_yd = at(x, y_up, z), at(x, y_dn, z)
    dev_xu, dev_xd = at(x_up, y, z), at(x_dn, y, z)
    send_w(0, wall.at[seg, core], 0, dev_yu)
    send_w(1, wall.at[seg, core], 1, dev_yd)
    send_w(2, wall.at[seg, core, 0], 4 + 2 * y, dev_xu)
    send_w(3, wall.at[seg, core, 1], 5 + 2 * y, dev_xd)

    def landed(ref, slot):
        pltpu.make_async_copy(ref, ref, wrs.at[slot]).wait()

    def spread(index, sec, sy):
        send_w(index, wall.at[sec, core, 0], 4 + 2 * sy, dev_xu)
        send_w(index + 1, wall.at[sec, core, 1], 5 + 2 * sy, dev_xd)
        send_w(index + 2, wall.at[sec, core], 12 + sec, partner)

    landed(wall.at[sec_dn, core], 0)
    send_w(4, wall.at[sec_dn, core, 0], 2, dev_yu)
    spread(5, sec_dn, y_dn)
    landed(wall.at[sec_up, core], 1)
    send_w(8, wall.at[sec_up, core, 1], 3, dev_yd)
    spread(9, sec_up, y_up)
    landed(wall.at[sec_far, core, 0], 2)
    landed(wall.at[sec_far, core, 1], 3)
    spread(12, sec_far, lax.rem(y + 2, 4))
    for j in range(4):
        sy = lax.rem(y + j, 4)
        sec = (1 - x_lo) * 4 + sy
        landed(wall.at[sec, core, 0], 4 + 2 * sy)
        landed(wall.at[sec, core, 1], 5 + 2 * sy)
        send_w(15 + j, wall.at[sec, core], 12 + sec, partner)
    for j in range(1, 8):
        sec = lax.rem(seg + j, 8)
        landed(wall.at[sec, other], 12 + sec)

    ones = (lax.broadcasted_iota(jnp.int32, (lanes - K3, W), 0) < 2).astype(F32).astype(BF)

    @pl.loop(0, APPS)
    def _(a):
        pbuf[a, K3:, :] = ones

    @pl.when(jnp.logical_not(has_up))
    def _():
        @pl.loop(0, APPS)
        def _(a):
            pbuf[a, 0:C, :] = jnp.zeros((C, W), BF)
            gbuf[a + 1, 0:C, :] = jnp.zeros((C, W), BF)

    @pl.when(jnp.logical_not(has_dn))
    def _():
        @pl.loop(0, APPS)
        def _(a):
            pbuf[a, C : 2 * C, :] = jnp.zeros((C, W), BF)
            gbuf[a + 1, C : 2 * C, :] = jnp.zeros((C, W), BF)

    @pl.when(odd == 1)
    def _():
        swap.wait()

    @pl.when(odd == 0)
    def _():
        xc[...] = x_ref[...]

    sbuf[0] = xc[0]
    gbuf[APPS, 2 * C :, :] = xc[1]

    def halo_copies(buf, slot, step):
        own = buf.at[slot, pl.ds(2 * C, C), :]
        to_up = remote(own, buf.at[slot, pl.ds(C, C), :], hss.at[step, 0], hrs.at[step, 1], up_dev)
        to_dn = remote(own, buf.at[slot, pl.ds(0, C), :], hss.at[step, 1], hrs.at[step, 0], dn_dev)
        return to_up, to_dn

    def halo_start(buf, slot, step):
        to_up, to_dn = halo_copies(buf, slot, step)

        @pl.when(has_up)
        def _():
            to_up.start()

        @pl.when(has_dn)
        def _():
            to_dn.start()

    def halo_wait(buf, slot, step):
        to_up, to_dn = halo_copies(buf, slot, step)

        @pl.when(has_up)
        def _():
            to_up.wait_send()
            pltpu.make_async_copy(buf.at[slot, pl.ds(0, C), :], buf.at[slot, pl.ds(0, C), :], hrs.at[step, 0]).wait()

        @pl.when(has_dn)
        def _():
            to_dn.wait_send()
            pltpu.make_async_copy(buf.at[slot, pl.ds(C, C), :], buf.at[slot, pl.ds(C, C), :], hrs.at[step, 1]).wait()

    out_slot = y * 2 + lax.rem(xr, 2)
    out_lat = 2 * z + xr // 2

    def out_copy(src, dst, which, k):
        dev = {"segment": k, "lat": out_lat, "dp": core}
        return remote(src, dst.at[out_slot], oss.at[which, k], ors.at[which, out_slot], dev)

    def is_self(k):
        return jnp.logical_and(seg == k, out_lat == lat)

    def out_send(src, dst, which, k):
        mine = is_self(k)

        @pl.when(mine)
        def _():
            dst[out_slot] = src[...]

        @pl.when(jnp.logical_not(mine))
        def _():
            out_copy(src, dst, which, k).start()

    def shifted_sum(parts, sign):
        minus, same, plus = parts[0:C], parts[C : 2 * C], parts[2 * C :]
        return same + pltpu.roll(minus, 1 if sign < 0 else W - 1, 1) + pltpu.roll(plus, W - 1 if sign < 0 else 1, 1)

    def forward(a, carry):
        k = lax.rem(a, SECTIONS)
        state = sbuf[a].astype(F32)
        pbuf[a, 2 * C : K3, :] = silu_value(state).astype(BF)
        halo_start(pbuf, a, a)
        own = jnp.dot(
            wall[k, :, :, :, 2 * C :].reshape(K3, lanes - 2 * C), pbuf[a, 2 * C :, :], preferred_element_type=F32
        )
        halo_wait(pbuf, a, a)
        rest = jnp.dot(
            wall[k, :, :, :, 0 : 2 * C].reshape(K3, 2 * C), pbuf[a, 0 : 2 * C, :], preferred_element_type=F32
        )
        sbuf[a + 1] = (state + shifted_sum(own + rest, -1)).astype(BF)

        @pl.when(a >= APPS - SECTIONS)
        def _():
            out_send(sbuf.at[a + 1], so_ref, 0, k)

        return carry

    lax.fori_loop(0, APPS, forward, 0)

    def turned_weights(k):
        for q in range(3):
            flat = wall[k].reshape(K3, lanes)[q * C : (q + 1) * C]
            turned = flat[:, : K3].T
            b2[1, q * C : (q + 1) * C, :] = turned[0:C]
            b2[0, q * C : (q + 1) * C, :] = turned[C : 2 * C]
            b2[2, q * C : (q + 1) * C, :] = turned[2 * C :]

    def tapped(grad):
        wide = grad.astype(F32)
        return jnp.concatenate(
            [pltpu.roll(wide, W - 1, 1).astype(BF), grad, pltpu.roll(wide, 1, 1).astype(BF)], axis=0
        )

    def reduce_pair(k):
        mine = dwf.at[k, core]
        pltpu.make_async_copy(cr.at[k], cr.at[k], crr.at[k]).wait()
        cs[k] = (mine[...].astype(F32) + cr[k].astype(F32)).astype(BF)

        @pl.when(seg == k)
        def _():
            r2[seg] = cs[k]

        @pl.when(seg != k)
        def _():
            remote(cs.at[k], r2.at[seg], r2s.at[k], r2r.at[seg], {"segment": k, "lat": lat, "dp": core}).start()

    def backward(a, with_weights):
        k = lax.rem(a, SECTIONS)
        step = APPS + APPS - 1 - a
        slot = a + 1
        halo_start(gbuf, slot, step)
        grad = gbuf[slot, 2 * C :, :]
        turned_weights(k)
        own = jnp.dot(b2[2], grad, preferred_element_type=F32)
        if with_weights:
            later = a + SECTIONS
            taps = jnp.concatenate([tapped(grad), tapped(gbuf[later + 1, 2 * C :, :])], axis=1)
            acts = jnp.concatenate([pbuf[a], pbuf[later]], axis=1)
            dw = lax.dot_general(taps, acts, (((1,), (1,)), ((), ())), preferred_element_type=F32)
            dwf[k] = dw.astype(BF).reshape(2, half, lanes)
            remote(dwf.at[k, other], cr.at[k], crs.at[k], crr.at[k], partner).start()

            @pl.when(a < SECTIONS - 1)
            def _():
                reduce_pair(k + 1)

        halo_wait(gbuf, slot, step)
        rest = jnp.dot(b2[0], gbuf[slot, 0:C, :], preferred_element_type=F32) + jnp.dot(
            b2[1], gbuf[slot, C : 2 * C, :], preferred_element_type=F32
        )
        slope = silu_slope(sbuf[a].astype(F32))
        adjoint = grad.astype(F32) + slope * shifted_sum(own + rest, 1)
        if not with_weights:
            adjoint = adjoint + jnp.where(a == SECTIONS, xc[2].astype(F32), 0.0)
        gbuf[a, 2 * C :, :] = adjoint.astype(BF)
        if with_weights:
            out_send(gbuf.at[a, pl.ds(2 * C, C), :], sa_ref, 1, k)

    def backward_late(i, carry):
        backward(APPS - 1 - i, False)
        return carry

    def backward_early(i, carry):
        backward(SECTIONS - 1 - i, True)
        return carry

    lax.fori_loop(0, SECTIONS, backward_late, 0)
    lax.fori_loop(0, SECTIONS, backward_early, 0)

    reduce_pair(0)
    total = cs[seg].astype(F32)
    for d in range(1, 8):
        src = lax.rem(seg + d, 8)
        pltpu.make_async_copy(r2.at[src], r2.at[src], r2r.at[src]).wait()
        total = total + r2[src].astype(F32)
    r3st[...] = total.astype(BF).reshape(nu, ur, lanes)
    for u in range(nu):
        @pl.when(lat != u)
        def _():
            remote(
                r3st.at[u], r3.at[lat], r3s.at[u], r3r.at[lat], {"segment": seg, "lat": u, "dp": core}
            ).start()

    @pl.when(lat < nu)
    def _():
        unit = r3st[lat].astype(F32)
        for d in range(1, nlat):
            src = lax.rem(lat + d, nlat)
            pltpu.make_async_copy(r3.at[src], r3.at[src], r3r.at[src]).wait()
            unit = unit + r3[src].astype(F32)
        gw_ref[core, lat] = unit.astype(BF)
        for d in range(1, nlat):
            peer = {"segment": seg, "lat": lax.rem(lat + d, nlat), "dp": core}
            remote(gw_ref.at[core, lat], gw_ref.at[core, lat], r4s.at[d], r4r.at[lat], peer).start()

    for u in range(nu):
        @pl.when(lat != u)
        def _():
            pltpu.make_async_copy(gw_ref.at[core, u], gw_ref.at[core, u], r4r.at[u]).wait()
    last = remote(gw_ref.at[core], gw_ref.at[core], r5.at[0], r5.at[1], partner)
    last.start()

    for copy in sends:
        copy.wait_send()
    for k in range(SECTIONS):
        for which, (dst, src) in enumerate(
            ((so_ref, sbuf.at[APPS - SECTIONS + k + 1]), (sa_ref, gbuf.at[k, pl.ds(2 * C, C), :]))
        ):
            @pl.when(jnp.logical_not(is_self(k)))
            def _():
                out_copy(src, dst, which, k).wait_send()

    for s in range(8):
        sxr = 2 * x_hi + s % 2
        sx = sxr + odd * (3 - 2 * sxr)
        from_self = jnp.logical_and(sx == x, y == s // 2)
        for which, dst in enumerate((so_ref, sa_ref)):
            @pl.when(jnp.logical_not(from_self))
            def _():
                pltpu.make_async_copy(dst.at[s], dst.at[s], ors.at[which, s]).wait()

    for k in range(SECTIONS):
        pltpu.make_async_copy(dwf.at[k, other], dwf.at[k, other], crs.at[k]).wait()

        @pl.when(seg != k)
        def _():
            pltpu.make_async_copy(cs.at[k], cs.at[k], r2s.at[k]).wait()

    for u in range(nu):
        @pl.when(lat != u)
        def _():
            pltpu.make_async_copy(r3st.at[u], r3st.at[u], r3s.at[u]).wait()

    @pl.when(lat < nu)
    def _():
        for d in range(1, nlat):
            pltpu.make_async_copy(gw_ref.at[core, lat], gw_ref.at[core, lat], r4s.at[d]).wait()

    last.wait_send()
    pltpu.make_async_copy(gw_ref.at[other], gw_ref.at[other], r5.at[1]).wait()


def per_device(nz, initial, kernel, bias, cotangent):
    seg = lax.axis_index("segment")
    x_lo, y = seg // 4, lax.rem(seg, 4)
    C, W = initial.shape[1], initial.shape[3]
    K3 = 3 * C
    lanes = -(-(K3 + 2) // 128) * 128
    half, part = K3 // 2, K3 // 4
    nlat = 2 * nz
    nu = units_for(nlat, half)
    ur = half // nu

    stacked = jnp.concatenate([initial[None], cotangent[1:2], cotangent[0:1]], axis=0)
    rows = lax.dynamic_slice(
        stacked, (0, y, 0, x_lo, 0), (3, 1, C, 1, W)
    ).reshape(3, C, W)

    taps = kernel[0].reshape(C, 3, 3, C)
    taps = jnp.concatenate([taps[:, 0:1], taps[:, 2:3], taps[:, 1:2]], axis=1)
    flat = taps.transpose(2, 0, 1, 3).reshape(K3, K3)
    coarse = lax.reduce_precision(bias[0], 8, 7)
    fine = bias[0] - coarse
    pair = jnp.stack([coarse, fine], axis=1).astype(BF)
    side = jnp.pad(pair, ((C, C), (0, lanes - K3 - 2)))
    weights = jnp.concatenate([flat, side], axis=1)

    vm = pl.BlockSpec(memory_space=pltpu.VMEM)
    dma = pltpu.SemaphoreType.DMA
    so, sa, gw = pl.pallas_call(
        functools.partial(network_kernel, (C, W, nz)),
        out_shape=(
            jax.ShapeDtypeStruct((8, C, W), BF),
            jax.ShapeDtypeStruct((8, C, W), BF),
            jax.ShapeDtypeStruct((2, nu, ur, lanes), BF),
        ),
        in_specs=[vm, vm],
        out_specs=(vm, vm, vm),
        scratch_shapes=[
            pltpu.VMEM((3, C, W), BF),
            pltpu.VMEM((SECTIONS, 2, 2, part, lanes), BF),
            pltpu.VMEM((3, K3, C), BF),
            pltpu.VMEM((APPS, lanes, W), BF),
            pltpu.VMEM((APPS + 1, K3, W), BF),
            pltpu.VMEM((APPS + 1, C, W), BF),
            pltpu.VMEM((SECTIONS, 2, half, lanes), BF),
            pltpu.VMEM((SECTIONS, half, lanes), BF),
            pltpu.VMEM((SECTIONS, half, lanes), BF),
            pltpu.VMEM((SECTIONS, half, lanes), BF),
            pltpu.VMEM((nu, ur, lanes), BF),
            pltpu.VMEM((nlat, ur, lanes), BF),
            dma((2,)),
            dma((19,)),
            dma((20,)),
            dma((2 * APPS, 2)),
            dma((2 * APPS, 2)),
            dma((2, SECTIONS)),
            dma((2, 8)),
            dma((SECTIONS,)),
            dma((SECTIONS,)),
            dma((SECTIONS,)),
            dma((SECTIONS,)),
            dma((nu,)),
            dma((nlat,)),
            dma((nlat,)),
            dma((nu,)),
            dma((2,)),
        ],
        compiler_params=pltpu.CompilerParams(
            collective_id=0, has_side_effects=True, vmem_limit_bytes=60 * 2**20
        ),
    )(rows, weights)

    def banded(slots):
        return slots.reshape(4, 2, C, W).transpose(0, 2, 1, 3)[None]

    normalizer = 1.0 / math.sqrt(initial.shape[0] * 2 * initial.shape[2] * nlat * W)
    grads = gw.reshape(K3, lanes).astype(F32) * normalizer
    core_grads = grads[:, :K3].reshape(3, C, 3, C).transpose(1, 2, 0, 3)
    core_grads = jnp.concatenate([core_grads[:, 0:1], core_grads[:, 2:3], core_grads[:, 1:2]], axis=1)
    return (
        banded(so),
        banded(sa).astype(F32),
        core_grads.reshape(1, C, 9, C),
        grads[C : 2 * C, K3][None],
    )


def solution(mesh):
    nz = mesh.shape["lat"] // 2
    return jax.shard_map(
        functools.partial(per_device, nz),
        mesh=mesh,
        in_specs=(
            P("dp", None, "lat", None),
            P("segment", None, None, None),
            P("segment", None),
            P(None, "dp", None, "lat", None),
        ),
        out_specs=(
            P("segment", "dp", None, "lat", None),
            P("segment", "dp", None, "lat", None),
            P("segment", None, None, None),
            P("segment", None),
        ),
        check_vma=False,
    )
```

```python
import functools
import math

import jax
import jax.numpy as jnp
from jax import lax
from jax.experimental import pallas as pl
from jax.experimental.pallas import tpu as pltpu
from jax.sharding import PartitionSpec as P

STEPS = 2
SECTIONS = 8
APPS = STEPS * SECTIONS
BF = jnp.bfloat16
F32 = jnp.float32
MESH = pl.DeviceIdType.MESH
HALO_UP, HALO_DN = 0, 1


def silu_value(values):
    return values / (1.0 + jnp.exp(-values))


def silu_slope(values):
    sigmoid_v = 1.0 / (1.0 + jnp.exp(-values))
    return sigmoid_v * (1.0 + values * (1.0 - sigmoid_v))


PIECES = 6
UNITS = 3


def network_kernel(
    dims, x_ref, w_ref, so_ref, sa_ref, gw_ref,
    xc, wall, b2, pbuf, gbuf, sbuf, dwf, cr, cs, r2, st2, r3, red, xsem, wss, wrs,
    hss, hrs, oss, ors, crs, crr, r2s, r2r, r3s, r3r, r4s, r4r, r5s, r5r, r6,
):
    C, W, nz = dims
    K3 = 3 * C
    half = K3 // 2
    part = half // 2
    lanes = w_ref.shape[1]
    nlat = 2 * nz
    nrow = 4 * nz
    piece = half // PIECES

    seg = lax.axis_index("segment")
    lat = lax.axis_index("lat")
    core = lax.axis_index("dp")
    x_lo, y = seg // 4, lax.rem(seg, 4)
    z, x_hi = lat // 2, lax.rem(lat, 2)
    x = 2 * x_hi + x_lo
    odd = lax.rem(z, 2)
    xr = x + odd * (3 - 2 * x)
    row = 4 * z + xr
    has_up = row > 0
    has_dn = row < nrow - 1

    def at(px, py, pz, pc=core):
        return {"segment": lax.rem(px, 2) * 4 + py, "lat": pz * 2 + px // 2, "dp": pc}

    def holder(r):
        rz = r // 4
        rx = lax.rem(r, 4)
        return at(rx + lax.rem(rz, 2) * (3 - 2 * rx), y, rz)

    up_dev = holder(jnp.maximum(row - 1, 0))
    dn_dev = holder(jnp.minimum(row + 1, nrow - 1))
    other = 1 - core
    partner = {"segment": seg, "lat": lat, "dp": other}
    y_up, y_dn = lax.rem(y + 1, 4), lax.rem(y + 3, 4)
    x_up, x_dn = lax.rem(x + 1, 4), lax.rem(x + 3, 4)

    barrier = pltpu.get_barrier_semaphore()
    for d in range(1, 16):
        dx, dy = d // 4, d % 4
        pl.semaphore_signal(
            barrier, inc=1, device_id=at(lax.rem(x + dx, 4), lax.rem(y + dy, 4), z), device_id_type=MESH
        )
    for d in range(1, nz):
        for hi in range(2):
            peer = {"segment": seg, "lat": lax.rem(z + d, nz) * 2 + hi, "dp": core}
            pl.semaphore_signal(barrier, inc=1, device_id=peer, device_id_type=MESH)
    pl.semaphore_signal(barrier, inc=1, device_id=partner, device_id_type=MESH)
    pl.semaphore_wait(barrier, 15 + 2 * (nz - 1) + 1)

    def remote(src, dst, ssem, rsem, dev):
        return pltpu.make_async_remote_copy(
            src_ref=src, dst_ref=dst, send_sem=ssem, recv_sem=rsem, device_id=dev, device_id_type=MESH
        )

    swap = remote(x_ref, xc, xsem.at[0], xsem.at[1], at(3 - x, y, z))

    @pl.when(odd == 1)
    def _():
        swap.start()

    wall[seg] = w_ref[...].reshape(2, 2, part, lanes)
    sec_dn, sec_up = x_lo * 4 + y_dn, x_lo * 4 + y_up
    sec_far = x_lo * 4 + lax.rem(y + 2, 4)
    sends = []

    def go(copy):
        copy.start()
        sends.append(copy)

    def send_w(index, src, slot, dev):
        go(remote(src, src, wss.at[index], wrs.at[slot], dev))

    dev_yu, dev_yd = at(x, y_up, z), at(x, y_dn, z)
    dev_xu, dev_xd = at(x_up, y, z), at(x_dn, y, z)
    send_w(0, wall.at[seg, core], 0, dev_yu)
    send_w(1, wall.at[seg, core], 1, dev_yd)
    send_w(2, wall.at[seg, core, 0], 4 + 2 * y, dev_xu)
    send_w(3, wall.at[seg, core, 1], 5 + 2 * y, dev_xd)

    def landed(ref, slot):
        pltpu.make_async_copy(ref, ref, wrs.at[slot]).wait()

    def spread(index, sec, sy):
        send_w(index, wall.at[sec, core, 0], 4 + 2 * sy, dev_xu)
        send_w(index + 1, wall.at[sec, core, 1], 5 + 2 * sy, dev_xd)
        send_w(index + 2, wall.at[sec, core], 12 + sec, partner)

    landed(wall.at[sec_dn, core], 0)
    send_w(4, wall.at[sec_dn, core, 0], 2, dev_yu)
    spread(5, sec_dn, y_dn)
    landed(wall.at[sec_up, core], 1)
    send_w(8, wall.at[sec_up, core, 1], 3, dev_yd)
    spread(9, sec_up, y_up)
    landed(wall.at[sec_far, core, 0], 2)
    landed(wall.at[sec_far, core, 1], 3)
    spread(12, sec_far, lax.rem(y + 2, 4))
    for j in range(4):
        sy = lax.rem(y + j, 4)
        sec = (1 - x_lo) * 4 + sy
        landed(wall.at[sec, core, 0], 4 + 2 * sy)
        landed(wall.at[sec, core, 1], 5 + 2 * sy)
        send_w(15 + j, wall.at[sec, core], 12 + sec, partner)
    for j in range(1, 8):
        sec = lax.rem(seg + j, 8)
        landed(wall.at[sec, other], 12 + sec)

    ones = (lax.broadcasted_iota(jnp.int32, (lanes - K3, W), 0) < 2).astype(F32).astype(BF)

    @pl.loop(0, APPS)
    def _(a):
        pbuf[a, K3:, :] = ones

    @pl.when(jnp.logical_not(has_up))
    def _():
        @pl.loop(0, APPS)
        def _(a):
            pbuf[a, 0:C, :] = jnp.zeros((C, W), BF)
            gbuf[a + 1, 0:C, :] = jnp.zeros((C, W), BF)

    @pl.when(jnp.logical_not(has_dn))
    def _():
        @pl.loop(0, APPS)
        def _(a):
            pbuf[a, C : 2 * C, :] = jnp.zeros((C, W), BF)
            gbuf[a + 1, C : 2 * C, :] = jnp.zeros((C, W), BF)

    @pl.when(odd == 1)
    def _():
        swap.wait()

    @pl.when(odd == 0)
    def _():
        xc[...] = x_ref[...]

    sbuf[0] = xc[0]
    gbuf[APPS, 2 * C :, :] = xc[1]

    def halo_copies(buf, slot, step):
        own = buf.at[slot, pl.ds(2 * C, C), :]
        to_up = remote(own, buf.at[slot, pl.ds(C, C), :], hss.at[step, 0], hrs.at[step, 1], up_dev)
        to_dn = remote(own, buf.at[slot, pl.ds(0, C), :], hss.at[step, 1], hrs.at[step, 0], dn_dev)
        return to_up, to_dn

    def halo_start(buf, slot, step):
        to_up, to_dn = halo_copies(buf, slot, step)

        @pl.when(has_up)
        def _():
            to_up.start()

        @pl.when(has_dn)
        def _():
            to_dn.start()

    def halo_wait(buf, slot, step):
        to_up, to_dn = halo_copies(buf, slot, step)

        @pl.when(has_up)
        def _():
            to_up.wait_send()
            pltpu.make_async_copy(buf.at[slot, pl.ds(0, C), :], buf.at[slot, pl.ds(0, C), :], hrs.at[step, 0]).wait()

        @pl.when(has_dn)
        def _():
            to_dn.wait_send()
            pltpu.make_async_copy(buf.at[slot, pl.ds(C, C), :], buf.at[slot, pl.ds(C, C), :], hrs.at[step, 1]).wait()

    out_slot = y * 2 + lax.rem(xr, 2)
    out_lat = 2 * z + xr // 2

    def out_copy(src, dst, which, k):
        dev = {"segment": k, "lat": out_lat, "dp": core}
        return remote(src, dst.at[out_slot], oss.at[which, k], ors.at[which, out_slot], dev)

    def is_self(k):
        return jnp.logical_and(seg == k, out_lat == lat)

    def out_send(src, dst, which, k):
        mine = is_self(k)

        @pl.when(mine)
        def _():
            dst[out_slot] = src[...]

        @pl.when(jnp.logical_not(mine))
        def _():
            out_copy(src, dst, which, k).start()

    def shifted_sum(parts, sign):
        minus, same, plus = parts[0:C], parts[C : 2 * C], parts[2 * C :]
        return same + pltpu.roll(minus, 1 if sign < 0 else W - 1, 1) + pltpu.roll(plus, W - 1 if sign < 0 else 1, 1)

    def forward(a, carry):
        k = lax.rem(a, SECTIONS)
        state = sbuf[a].astype(F32)
        pbuf[a, 2 * C : K3, :] = silu_value(state).astype(BF)
        halo_start(pbuf, a, a)
        own = jnp.dot(
            wall[k, :, :, :, 2 * C :].reshape(K3, lanes - 2 * C), pbuf[a, 2 * C :, :], preferred_element_type=F32
        )
        halo_wait(pbuf, a, a)
        rest = jnp.dot(
            wall[k, :, :, :, 0 : 2 * C].reshape(K3, 2 * C), pbuf[a, 0 : 2 * C, :], preferred_element_type=F32
        )
        sbuf[a + 1] = (state + shifted_sum(own + rest, -1)).astype(BF)

        @pl.when(a >= APPS - SECTIONS)
        def _():
            out_send(sbuf.at[a + 1], so_ref, 0, k)

        return carry

    lax.fori_loop(0, APPS, forward, 0)

    def turned_weights(k):
        for q in range(3):
            flat = wall[k].reshape(K3, lanes)[q * C : (q + 1) * C]
            turned = flat[:, : K3].T
            b2[1, q * C : (q + 1) * C, :] = turned[0:C]
            b2[0, q * C : (q + 1) * C, :] = turned[C : 2 * C]
            b2[2, q * C : (q + 1) * C, :] = turned[2 * C :]

    def tapped(grad):
        wide = grad.astype(F32)
        return jnp.concatenate(
            [pltpu.roll(wide, W - 1, 1).astype(BF), grad, pltpu.roll(wide, 1, 1).astype(BF)], axis=0
        )

    def pair_and_scatter(k):
        pltpu.make_async_copy(cr.at[k], cr.at[k], crr.at[k]).wait()
        for jx in range(2):
            for jy in range(3):
                j = 3 * jx + jy
                cs[k, j] = (dwf[k, core, j].astype(F32) + cr[k, j].astype(F32)).astype(BF)
                near = x_lo == jx
                far_x = lax.rem(x + (1 if jy % 2 == 0 else 3), 4)
                home = at(jnp.where(near, x, far_x), jy, z)
                slot = jnp.where(near, y, 4 + y)
                mine = jnp.logical_and(near, y == jy)

                @pl.when(mine)
                def _():
                    r2[k, slot] = cs[k, j]

                @pl.when(jnp.logical_not(mine))
                def _():
                    remote(cs.at[k, j], r2.at[k, slot], r2s.at[k, j], r2r.at[k, slot], home).start()

    def unit_lat(k, u):
        return lax.rem((nlat // 3) * u + 2 * k, nlat)

    def sum_and_scatter(k):
        @pl.when(y < 3)
        def _():
            total = r2[k, y].astype(F32)
            for d in range(1, 4):
                src = lax.rem(y + d, 4)
                pltpu.make_async_copy(r2.at[k, src], r2.at[k, src], r2r.at[k, src]).wait()
                total = total + r2[k, src].astype(F32)
            for src in range(4, 8):
                pltpu.make_async_copy(r2.at[k, src], r2.at[k, src], r2r.at[k, src]).wait()
                total = total + r2[k, src].astype(F32)
            st2[k] = total.astype(BF).reshape(UNITS, piece // UNITS, lanes)
            for u in range(UNITS):
                goal = unit_lat(k, u)

                @pl.when(goal != lat)
                def _():
                    dev = {"segment": seg, "lat": goal, "dp": core}
                    remote(st2.at[k, u], r3.at[k, lat], r3s.at[k, u], r3r.at[k, lat], dev).start()

    def lat_sum(k):
        for u in range(UNITS):
            @pl.when(jnp.logical_and(y < 3, unit_lat(k, u) == lat))
            def _():
                unit = st2[k, u].astype(F32)
                for d in range(1, nlat):
                    src = lax.rem(lat + d, nlat)
                    pltpu.make_async_copy(r3.at[k, src], r3.at[k, src], r3r.at[k, src]).wait()
                    unit = unit + r3[k, src].astype(F32)
                red[k, u] = unit.astype(BF)
                for d in range(1, nlat):
                    dev = {"segment": seg, "lat": lax.rem(lat + d, nlat), "dp": core}
                    remote(red.at[k, u], red.at[k, u], r4s.at[k, d], r4r.at[k, u], dev).start()

    my_piece = 3 * x_lo + jnp.minimum(y, 2)

    def deliver(k):
        @pl.when(y < 3)
        def _():
            for u in range(UNITS):
                @pl.when(unit_lat(k, u) != lat)
                def _():
                    pltpu.make_async_copy(red.at[k, u], red.at[k, u], r4r.at[k, u]).wait()

            @pl.when(seg == k)
            def _():
                gw_ref[core, my_piece] = red[k]

            @pl.when(seg != k)
            def _():
                dev = {"segment": k, "lat": lat, "dp": core}
                remote(red.at[k], gw_ref.at[core, my_piece], r5s.at[k], r5r.at[my_piece], dev).start()

    def staged(a):
        for lag, stage in ((1, pair_and_scatter), (3, sum_and_scatter), (5, lat_sum), (7, deliver)):
            k = a + lag

            @pl.when(jnp.logical_and(k >= 0, k < SECTIONS))
            def _():
                stage(k)

    def backward(a, with_weights):
        k = lax.rem(a, SECTIONS)
        step = APPS + APPS - 1 - a
        slot = a + 1
        halo_start(gbuf, slot, step)
        grad = gbuf[slot, 2 * C :, :]
        turned_weights(k)
        own = jnp.dot(b2[2], grad, preferred_element_type=F32)
        if with_weights:
            later = a + SECTIONS
            taps = jnp.concatenate([tapped(grad), tapped(gbuf[later + 1, 2 * C :, :])], axis=1)
            acts = jnp.concatenate([pbuf[a], pbuf[later]], axis=1)
            dw = lax.dot_general(taps, acts, (((1,), (1,)), ((), ())), preferred_element_type=F32)
            dwf[k] = dw.astype(BF).reshape(2, PIECES, piece, lanes)
            remote(dwf.at[k, other], cr.at[k], crs.at[k], crr.at[k], partner).start()
            staged(a)

        halo_wait(gbuf, slot, step)
        rest = jnp.dot(b2[0], gbuf[slot, 0:C, :], preferred_element_type=F32) + jnp.dot(
            b2[1], gbuf[slot, C : 2 * C, :], preferred_element_type=F32
        )
        slope = silu_slope(sbuf[a].astype(F32))
        adjoint = grad.astype(F32) + slope * shifted_sum(own + rest, 1)
        if not with_weights:
            adjoint = adjoint + jnp.where(a == SECTIONS, xc[2].astype(F32), 0.0)
        gbuf[a, 2 * C :, :] = adjoint.astype(BF)
        if with_weights:
            out_send(gbuf.at[a, pl.ds(2 * C, C), :], sa_ref, 1, k)

    def backward_late(i, carry):
        backward(APPS - 1 - i, False)
        return carry

    def backward_early(i, carry):
        backward(SECTIONS - 1 - i, True)
        return carry

    lax.fori_loop(0, SECTIONS, backward_late, 0)
    lax.fori_loop(0, SECTIONS, backward_early, 0)

    def drain(i, carry):
        staged(-1 - i)
        return carry

    lax.fori_loop(0, 7, drain, 0)
    for j in range(PIECES):
        @pl.when(seg != (j // 3) * 4 + j % 3)
        def _():
            pltpu.make_async_copy(gw_ref.at[core, j], gw_ref.at[core, j], r5r.at[j]).wait()
    last = remote(gw_ref.at[core], gw_ref.at[core], r6.at[0], r6.at[1], partner)
    last.start()

    for copy in sends:
        copy.wait_send()
    for k in range(SECTIONS):
        for which, (dst, src) in enumerate(
            ((so_ref, sbuf.at[APPS - SECTIONS + k + 1]), (sa_ref, gbuf.at[k, pl.ds(2 * C, C), :]))
        ):
            @pl.when(jnp.logical_not(is_self(k)))
            def _():
                out_copy(src, dst, which, k).wait_send()

    for s in range(8):
        sxr = 2 * x_hi + s % 2
        sx = sxr + odd * (3 - 2 * sxr)
        from_self = jnp.logical_and(sx == x, y == s // 2)
        for which, dst in enumerate((so_ref, sa_ref)):
            @pl.when(jnp.logical_not(from_self))
            def _():
                pltpu.make_async_copy(dst.at[s], dst.at[s], ors.at[which, s]).wait()

    def ended(k, carry):
        pltpu.make_async_copy(dwf.at[k, other], dwf.at[k, other], crs.at[k]).wait()
        for j in range(PIECES):
            @pl.when(seg != (j // 3) * 4 + j % 3)
            def _():
                pltpu.make_async_copy(cs.at[k, j], cs.at[k, j], r2s.at[k, j]).wait()

        @pl.when(y < 3)
        def _():
            for u in range(UNITS):
                mine = unit_lat(k, u) == lat

                @pl.when(jnp.logical_not(mine))
                def _():
                    pltpu.make_async_copy(st2.at[k, u], st2.at[k, u], r3s.at[k, u]).wait()

                @pl.when(mine)
                def _():
                    for d in range(1, nlat):
                        pltpu.make_async_copy(red.at[k, u], red.at[k, u], r4s.at[k, d]).wait()

            @pl.when(seg != k)
            def _():
                pltpu.make_async_copy(red.at[k], red.at[k], r5s.at[k]).wait()

        return carry

    lax.fori_loop(0, SECTIONS, ended, 0)
    last.wait_send()
    pltpu.make_async_copy(gw_ref.at[other], gw_ref.at[other], r6.at[1]).wait()


def per_device(nz, initial, kernel, bias, cotangent):
    seg = lax.axis_index("segment")
    x_lo, y = seg // 4, lax.rem(seg, 4)
    C, W = initial.shape[1], initial.shape[3]
    K3 = 3 * C
    lanes = -(-(K3 + 2) // 128) * 128
    half, part = K3 // 2, K3 // 4
    nlat = 2 * nz
    piece = half // PIECES
    unit = piece // UNITS

    stacked = jnp.concatenate([initial[None], cotangent[1:2], cotangent[0:1]], axis=0)
    rows = lax.dynamic_slice(
        stacked, (0, y, 0, x_lo, 0), (3, 1, C, 1, W)
    ).reshape(3, C, W)

    taps = kernel[0].reshape(C, 3, 3, C)
    taps = jnp.concatenate([taps[:, 0:1], taps[:, 2:3], taps[:, 1:2]], axis=1)
    flat = taps.transpose(2, 0, 1, 3).reshape(K3, K3)
    coarse = lax.reduce_precision(bias[0], 8, 7)
    fine = bias[0] - coarse
    pair = jnp.stack([coarse, fine], axis=1).astype(BF)
    side = jnp.pad(pair, ((C, C), (0, lanes - K3 - 2)))
    weights = jnp.concatenate([flat, side], axis=1)

    vm = pl.BlockSpec(memory_space=pltpu.VMEM)
    dma = pltpu.SemaphoreType.DMA
    so, sa, gw = pl.pallas_call(
        functools.partial(network_kernel, (C, W, nz)),
        out_shape=(
            jax.ShapeDtypeStruct((8, C, W), BF),
            jax.ShapeDtypeStruct((8, C, W), BF),
            jax.ShapeDtypeStruct((2, PIECES, UNITS, unit, lanes), BF),
        ),
        in_specs=[vm, vm],
        out_specs=(vm, vm, vm),
        scratch_shapes=[
            pltpu.VMEM((3, C, W), BF),
            pltpu.VMEM((SECTIONS, 2, 2, part, lanes), BF),
            pltpu.VMEM((3, K3, C), BF),
            pltpu.VMEM((APPS, lanes, W), BF),
            pltpu.VMEM((APPS + 1, K3, W), BF),
            pltpu.VMEM((APPS + 1, C, W), BF),
            pltpu.VMEM((SECTIONS, 2, PIECES, piece, lanes), BF),
            pltpu.VMEM((SECTIONS, PIECES, piece, lanes), BF),
            pltpu.VMEM((SECTIONS, PIECES, piece, lanes), BF),
            pltpu.VMEM((SECTIONS, 8, piece, lanes), BF),
            pltpu.VMEM((SECTIONS, UNITS, unit, lanes), BF),
            pltpu.VMEM((SECTIONS, nlat, unit, lanes), BF),
            pltpu.VMEM((SECTIONS, UNITS, unit, lanes), BF),
            dma((2,)),
            dma((19,)),
            dma((20,)),
            dma((2 * APPS, 2)),
            dma((2 * APPS, 2)),
            dma((2, SECTIONS)),
            dma((2, 8)),
            dma((SECTIONS,)),
            dma((SECTIONS,)),
            dma((SECTIONS, PIECES)),
            dma((SECTIONS, 8)),
            dma((SECTIONS, UNITS)),
            dma((SECTIONS, nlat)),
            dma((SECTIONS, nlat)),
            dma((SECTIONS, UNITS)),
            dma((SECTIONS,)),
            dma((PIECES,)),
            dma((2,)),
        ],
        compiler_params=pltpu.CompilerParams(
            collective_id=0, has_side_effects=True, vmem_limit_bytes=60 * 2**20
        ),
    )(rows, weights)

    def banded(slots):
        return slots.reshape(4, 2, C, W).transpose(0, 2, 1, 3)[None]

    normalizer = 1.0 / math.sqrt(initial.shape[0] * 2 * initial.shape[2] * nlat * W)
    grads = gw.reshape(K3, lanes).astype(F32) * normalizer
    core_grads = grads[:, :K3].reshape(3, C, 3, C).transpose(1, 2, 0, 3)
    core_grads = jnp.concatenate([core_grads[:, 0:1], core_grads[:, 2:3], core_grads[:, 1:2]], axis=1)
    return (
        banded(so),
        banded(sa).astype(F32),
        core_grads.reshape(1, C, 9, C),
        grads[C : 2 * C, K3][None],
    )


def solution(mesh):
    nz = mesh.shape["lat"] // 2
    return jax.shard_map(
        functools.partial(per_device, nz),
        mesh=mesh,
        in_specs=(
            P("dp", None, "lat", None),
            P("segment", None, None, None),
            P("segment", None),
            P(None, "dp", None, "lat", None),
        ),
        out_specs=(
            P("segment", "dp", None, "lat", None),
            P("segment", "dp", None, "lat", None),
            P("segment", None, None, None),
            P("segment", None),
        ),
        check_vma=False,
    )
```

```python
import functools
import math

import jax
import jax.numpy as jnp
from jax import lax
from jax.experimental import pallas as pl
from jax.experimental.pallas import tpu as pltpu
from jax.sharding import PartitionSpec as P

STEPS = 2
SECTIONS = 8
APPS = STEPS * SECTIONS
BF = jnp.bfloat16
F32 = jnp.float32
MESH = pl.DeviceIdType.MESH
HALO_UP, HALO_DN = 0, 1


def silu_value(values):
    return values / (1.0 + jnp.exp(-values))


def silu_slope(values):
    sigmoid_v = 1.0 / (1.0 + jnp.exp(-values))
    return sigmoid_v * (1.0 + values * (1.0 - sigmoid_v))


PIECES = 6
UNITS = 3


def network_kernel(
    dims, x_ref, w_ref, so_ref, sa_ref, gw_ref,
    xc, wall, b2, pbuf, gbuf, sbuf, dwf, cr, cs, r2, st2, r3, red, xsem, wss, wrs,
    hss, hrs, oss, ors, crs, crr, r2s, r2r, r3s, r3r, r4s, r4r, r5s, r5r, r6,
):
    C, W, nz = dims
    K3 = 3 * C
    half = K3 // 2
    part = half // 2
    lanes = w_ref.shape[1]
    nlat = 2 * nz
    nrow = 4 * nz
    piece = half // PIECES

    seg = lax.axis_index("segment")
    lat = lax.axis_index("lat")
    core = lax.axis_index("dp")
    x_lo, y = seg // 4, lax.rem(seg, 4)
    z, x_hi = lat // 2, lax.rem(lat, 2)
    x = 2 * x_hi + x_lo
    odd = lax.rem(z, 2)
    held = lax.rem(x_lo + x_hi, 2)
    band = 2 * z + lax.rem(x_hi + odd, 2)
    row = 2 * band + core
    has_up = row > 0
    has_dn = row < nrow - 1

    def at(px, py, pz, pc=core):
        return {"segment": lax.rem(px, 2) * 4 + py, "lat": pz * 2 + px // 2, "dp": pc}

    def holder(r):
        r_band = r // 2
        rz = r_band // 2
        hi = lax.rem(r_band + rz, 2)
        return {"segment": lax.rem(held + hi, 2) * 4 + y, "lat": rz * 2 + hi, "dp": lax.rem(r, 2)}

    up_dev = holder(jnp.maximum(row - 1, 0))
    dn_dev = holder(jnp.minimum(row + 1, nrow - 1))
    other = 1 - core
    partner = {"segment": seg, "lat": lat, "dp": other}
    y_up, y_dn = lax.rem(y + 1, 4), lax.rem(y + 3, 4)
    x_up, x_dn = lax.rem(x + 1, 4), lax.rem(x + 3, 4)

    barrier = pltpu.get_barrier_semaphore()
    for d in range(1, 32):
        dx, dy, dc = d // 8, (d // 2) % 4, d % 2
        peer = at(lax.rem(x + dx, 4), lax.rem(y + dy, 4), z, lax.rem(core + dc, 2))
        pl.semaphore_signal(barrier, inc=1, device_id=peer, device_id_type=MESH)
    for d in range(1, nz):
        for hi in range(2):
            peer = {"segment": seg, "lat": lax.rem(z + d, nz) * 2 + hi, "dp": core}
            pl.semaphore_signal(barrier, inc=1, device_id=peer, device_id_type=MESH)
    for d in (1, nz - 1):
        peer = {"segment": seg, "lat": lax.rem(z + d, nz) * 2 + x_hi, "dp": other}
        pl.semaphore_signal(barrier, inc=1, device_id=peer, device_id_type=MESH)
    pl.semaphore_wait(barrier, 31 + 2 * (nz - 1) + 2)

    def remote(src, dst, ssem, rsem, dev):
        return pltpu.make_async_remote_copy(
            src_ref=src, dst_ref=dst, send_sem=ssem, recv_sem=rsem, device_id=dev, device_id_type=MESH
        )

    giver = core == held
    stays = jnp.logical_and(giver, odd == 0)
    home_x = x + odd * (3 - 2 * x)

    def given(r, what):
        span = pl.ds(0, 1) if what == 0 else pl.ds(1, 2)
        return remote(
            x_ref.at[r, span], xc.at[span], xsem.at[0, 2 * r + what], xsem.at[1, what], at(home_x, y, z, r)
        )

    def leaves(r):
        return jnp.logical_and(giver, jnp.logical_or(odd == 1, core != r))

    for what in range(2):
        for r in range(2):
            @pl.when(leaves(r))
            def _():
                given(r, what).start()

    @pl.when(stays)
    def _():
        xc[...] = x_ref[core]

    def rows_wait(what):
        span = pl.ds(0, 1) if what == 0 else pl.ds(1, 2)

        @pl.when(jnp.logical_not(stays))
        def _():
            pltpu.make_async_copy(xc.at[span], xc.at[span], xsem.at[1, what]).wait()

    wall[seg] = w_ref[...].reshape(2, 2, part, lanes)
    sec_dn, sec_up = x_lo * 4 + y_dn, x_lo * 4 + y_up
    sec_far = x_lo * 4 + lax.rem(y + 2, 4)
    sends = []

    def go(copy):
        copy.start()
        sends.append(copy)

    def send_w(index, src, slot, dev):
        go(remote(src, src, wss.at[index], wrs.at[slot], dev))

    dev_yu, dev_yd = at(x, y_up, z), at(x, y_dn, z)
    dev_xu, dev_xd = at(x_up, y, z), at(x_dn, y, z)
    send_w(0, wall.at[seg, core], 0, dev_yu)
    send_w(1, wall.at[seg, core], 1, dev_yd)
    send_w(2, wall.at[seg, core, 0], 4 + 2 * y, dev_xu)
    send_w(3, wall.at[seg, core, 1], 5 + 2 * y, dev_xd)

    def landed(ref, slot):
        pltpu.make_async_copy(ref, ref, wrs.at[slot]).wait()

    def spread(index, sec, sy):
        send_w(index, wall.at[sec, core, 0], 4 + 2 * sy, dev_xu)
        send_w(index + 1, wall.at[sec, core, 1], 5 + 2 * sy, dev_xd)
        send_w(index + 2, wall.at[sec, core], 12 + sec, partner)

    landed(wall.at[sec_dn, core], 0)
    send_w(4, wall.at[sec_dn, core, 0], 2, dev_yu)
    spread(5, sec_dn, y_dn)
    landed(wall.at[sec_up, core], 1)
    send_w(8, wall.at[sec_up, core, 1], 3, dev_yd)
    spread(9, sec_up, y_up)
    landed(wall.at[sec_far, core, 0], 2)
    landed(wall.at[sec_far, core, 1], 3)
    spread(12, sec_far, lax.rem(y + 2, 4))
    for j in range(4):
        sy = lax.rem(y + j, 4)
        sec = (1 - x_lo) * 4 + sy
        landed(wall.at[sec, core, 0], 4 + 2 * sy)
        landed(wall.at[sec, core, 1], 5 + 2 * sy)
        send_w(15 + j, wall.at[sec, core], 12 + sec, partner)
    for j in range(1, 8):
        sec = lax.rem(seg + j, 8)
        landed(wall.at[sec, other], 12 + sec)

    ones = (lax.broadcasted_iota(jnp.int32, (lanes - K3, W), 0) < 2).astype(F32).astype(BF)

    @pl.loop(0, APPS)
    def _(a):
        pbuf[a, K3:, :] = ones

    @pl.when(jnp.logical_not(has_up))
    def _():
        @pl.loop(0, APPS)
        def _(a):
            pbuf[a, 0:C, :] = jnp.zeros((C, W), BF)
            gbuf[a + 1, 0:C, :] = jnp.zeros((C, W), BF)

    @pl.when(jnp.logical_not(has_dn))
    def _():
        @pl.loop(0, APPS)
        def _(a):
            pbuf[a, C : 2 * C, :] = jnp.zeros((C, W), BF)
            gbuf[a + 1, C : 2 * C, :] = jnp.zeros((C, W), BF)

    rows_wait(0)
    sbuf[0] = xc[0]

    def halo_copies(buf, slot, step):
        own = buf.at[slot, pl.ds(2 * C, C), :]
        to_up = remote(own, buf.at[slot, pl.ds(C, C), :], hss.at[step, 0], hrs.at[step, 1], up_dev)
        to_dn = remote(own, buf.at[slot, pl.ds(0, C), :], hss.at[step, 1], hrs.at[step, 0], dn_dev)
        return to_up, to_dn

    def halo_start(buf, slot, step):
        to_up, to_dn = halo_copies(buf, slot, step)

        @pl.when(has_up)
        def _():
            to_up.start()

        @pl.when(has_dn)
        def _():
            to_dn.start()

    def halo_wait(buf, slot, step):
        to_up, to_dn = halo_copies(buf, slot, step)

        @pl.when(has_up)
        def _():
            to_up.wait_send()
            pltpu.make_async_copy(buf.at[slot, pl.ds(0, C), :], buf.at[slot, pl.ds(0, C), :], hrs.at[step, 0]).wait()

        @pl.when(has_dn)
        def _():
            to_dn.wait_send()
            pltpu.make_async_copy(buf.at[slot, pl.ds(C, C), :], buf.at[slot, pl.ds(C, C), :], hrs.at[step, 1]).wait()

    out_slot = y * 2 + core

    def out_copy(src, dst, which, k):
        dev = {"segment": k, "lat": band, "dp": held}
        return remote(src, dst.at[out_slot], oss.at[which, k], ors.at[which, out_slot], dev)

    def is_self(k):
        return jnp.logical_and(seg == k, stays)

    def out_send(src, dst, which, k):
        mine = is_self(k)

        @pl.when(mine)
        def _():
            dst[out_slot] = src[...]

        @pl.when(jnp.logical_not(mine))
        def _():
            out_copy(src, dst, which, k).start()

    def shifted_sum(parts, sign):
        minus, same, plus = parts[0:C], parts[C : 2 * C], parts[2 * C :]
        return same + pltpu.roll(minus, 1 if sign < 0 else W - 1, 1) + pltpu.roll(plus, W - 1 if sign < 0 else 1, 1)

    def forward(a, carry):
        k = lax.rem(a, SECTIONS)
        state = sbuf[a].astype(F32)
        pbuf[a, 2 * C : K3, :] = silu_value(state).astype(BF)
        halo_start(pbuf, a, a)
        own = jnp.dot(
            wall[k, :, :, :, 2 * C :].reshape(K3, lanes - 2 * C), pbuf[a, 2 * C :, :], preferred_element_type=F32
        )
        halo_wait(pbuf, a, a)
        rest = jnp.dot(
            wall[k, :, :, :, 0 : 2 * C].reshape(K3, 2 * C), pbuf[a, 0 : 2 * C, :], preferred_element_type=F32
        )
        sbuf[a + 1] = (state + shifted_sum(own + rest, -1)).astype(BF)

        @pl.when(a >= APPS - SECTIONS)
        def _():
            out_send(sbuf.at[a + 1], so_ref, 0, k)

        return carry

    lax.fori_loop(0, APPS, forward, 0)

    rows_wait(1)
    gbuf[APPS, 2 * C :, :] = xc[1]

    def turned_weights(k):
        for q in range(3):
            flat = wall[k].reshape(K3, lanes)[q * C : (q + 1) * C]
            turned = flat[:, : K3].T
            b2[1, q * C : (q + 1) * C, :] = turned[0:C]
            b2[0, q * C : (q + 1) * C, :] = turned[C : 2 * C]
            b2[2, q * C : (q + 1) * C, :] = turned[2 * C :]

    def tapped(grad):
        wide = grad.astype(F32)
        return jnp.concatenate(
            [pltpu.roll(wide, W - 1, 1).astype(BF), grad, pltpu.roll(wide, 1, 1).astype(BF)], axis=0
        )

    def pair_and_scatter(k):
        pltpu.make_async_copy(cr.at[k], cr.at[k], crr.at[k]).wait()
        for jx in range(2):
            for jy in range(3):
                j = 3 * jx + jy
                cs[k, j] = (dwf[k, core, j].astype(F32) + cr[k, j].astype(F32)).astype(BF)
                near = x_lo == jx
                far_x = lax.rem(x + (1 if jy % 2 == 0 else 3), 4)
                home = at(jnp.where(near, x, far_x), jy, z)
                slot = jnp.where(near, y, 4 + y)
                mine = jnp.logical_and(near, y == jy)

                @pl.when(mine)
                def _():
                    r2[k, slot] = cs[k, j]

                @pl.when(jnp.logical_not(mine))
                def _():
                    remote(cs.at[k, j], r2.at[k, slot], r2s.at[k, j], r2r.at[k, slot], home).start()

    def unit_lat(k, u):
        return lax.rem((nlat // 3) * u + 2 * k, nlat)

    def sum_and_scatter(k):
        @pl.when(y < 3)
        def _():
            total = r2[k, y].astype(F32)
            for d in range(1, 4):
                src = lax.rem(y + d, 4)
                pltpu.make_async_copy(r2.at[k, src], r2.at[k, src], r2r.at[k, src]).wait()
                total = total + r2[k, src].astype(F32)
            for src in range(4, 8):
                pltpu.make_async_copy(r2.at[k, src], r2.at[k, src], r2r.at[k, src]).wait()
                total = total + r2[k, src].astype(F32)
            st2[k] = total.astype(BF).reshape(UNITS, piece // UNITS, lanes)
            for u in range(UNITS):
                goal = unit_lat(k, u)

                @pl.when(goal != lat)
                def _():
                    dev = {"segment": seg, "lat": goal, "dp": core}
                    remote(st2.at[k, u], r3.at[k, lat], r3s.at[k, u], r3r.at[k, lat], dev).start()

    def lat_sum(k):
        for u in range(UNITS):
            @pl.when(jnp.logical_and(y < 3, unit_lat(k, u) == lat))
            def _():
                unit = st2[k, u].astype(F32)
                for d in range(1, nlat):
                    src = lax.rem(lat + d, nlat)
                    pltpu.make_async_copy(r3.at[k, src], r3.at[k, src], r3r.at[k, src]).wait()
                    unit = unit + r3[k, src].astype(F32)
                red[k, u] = unit.astype(BF)
                for d in range(1, nlat):
                    dev = {"segment": seg, "lat": lax.rem(lat + d, nlat), "dp": core}
                    remote(red.at[k, u], red.at[k, u], r4s.at[k, d], r4r.at[k, u], dev).start()

    my_piece = 3 * x_lo + jnp.minimum(y, 2)

    def deliver(k):
        @pl.when(y < 3)
        def _():
            for u in range(UNITS):
                @pl.when(unit_lat(k, u) != lat)
                def _():
                    pltpu.make_async_copy(red.at[k, u], red.at[k, u], r4r.at[k, u]).wait()

            @pl.when(seg == k)
            def _():
                gw_ref[core, my_piece] = red[k]

            @pl.when(seg != k)
            def _():
                dev = {"segment": k, "lat": lat, "dp": core}
                remote(red.at[k], gw_ref.at[core, my_piece], r5s.at[k], r5r.at[my_piece], dev).start()

    def staged(a):
        for lag, stage in ((1, pair_and_scatter), (3, sum_and_scatter), (5, lat_sum), (7, deliver)):
            k = a + lag

            @pl.when(jnp.logical_and(k >= 0, k < SECTIONS))
            def _():
                stage(k)

    def backward(a, with_weights):
        k = lax.rem(a, SECTIONS)
        step = APPS + APPS - 1 - a
        slot = a + 1
        halo_start(gbuf, slot, step)
        grad = gbuf[slot, 2 * C :, :]
        turned_weights(k)
        own = jnp.dot(b2[2], grad, preferred_element_type=F32)
        if with_weights:
            later = a + SECTIONS
            taps = jnp.concatenate([tapped(grad), tapped(gbuf[later + 1, 2 * C :, :])], axis=1)
            acts = jnp.concatenate([pbuf[a], pbuf[later]], axis=1)
            dw = lax.dot_general(taps, acts, (((1,), (1,)), ((), ())), preferred_element_type=F32)
            dwf[k] = dw.astype(BF).reshape(2, PIECES, piece, lanes)
            remote(dwf.at[k, other], cr.at[k], crs.at[k], crr.at[k], partner).start()
            staged(a)

        halo_wait(gbuf, slot, step)
        rest = jnp.dot(b2[0], gbuf[slot, 0:C, :], preferred_element_type=F32) + jnp.dot(
            b2[1], gbuf[slot, C : 2 * C, :], preferred_element_type=F32
        )
        slope = silu_slope(sbuf[a].astype(F32))
        adjoint = grad.astype(F32) + slope * shifted_sum(own + rest, 1)
        if not with_weights:
            adjoint = adjoint + jnp.where(a == SECTIONS, xc[2].astype(F32), 0.0)
        gbuf[a, 2 * C :, :] = adjoint.astype(BF)
        if with_weights:
            out_send(gbuf.at[a, pl.ds(2 * C, C), :], sa_ref, 1, k)

    def backward_late(i, carry):
        backward(APPS - 1 - i, False)
        return carry

    def backward_early(i, carry):
        backward(SECTIONS - 1 - i, True)
        return carry

    lax.fori_loop(0, SECTIONS, backward_late, 0)
    lax.fori_loop(0, SECTIONS, backward_early, 0)

    def drain(i, carry):
        staged(-1 - i)
        return carry

    lax.fori_loop(0, 7, drain, 0)
    for j in range(PIECES):
        @pl.when(seg != (j // 3) * 4 + j % 3)
        def _():
            pltpu.make_async_copy(gw_ref.at[core, j], gw_ref.at[core, j], r5r.at[j]).wait()
    last = remote(gw_ref.at[core], gw_ref.at[core], r6.at[0], r6.at[1], partner)
    last.start()

    for copy in sends:
        copy.wait_send()
    for k in range(SECTIONS):
        for which, (dst, src) in enumerate(
            ((so_ref, sbuf.at[APPS - SECTIONS + k + 1]), (sa_ref, gbuf.at[k, pl.ds(2 * C, C), :]))
        ):
            @pl.when(jnp.logical_not(is_self(k)))
            def _():
                out_copy(src, dst, which, k).wait_send()

    for what in range(2):
        for r in range(2):
            @pl.when(leaves(r))
            def _():
                given(r, what).wait_send()

    for s in range(8):
        from_self = jnp.logical_and(stays, jnp.logical_and(core == s % 2, y == s // 2))
        for which, dst in enumerate((so_ref, sa_ref)):
            @pl.when(jnp.logical_not(from_self))
            def _():
                pltpu.make_async_copy(dst.at[s], dst.at[s], ors.at[which, s]).wait()

    def ended(k, carry):
        pltpu.make_async_copy(dwf.at[k, other], dwf.at[k, other], crs.at[k]).wait()
        for j in range(PIECES):
            @pl.when(seg != (j // 3) * 4 + j % 3)
            def _():
                pltpu.make_async_copy(cs.at[k, j], cs.at[k, j], r2s.at[k, j]).wait()

        @pl.when(y < 3)
        def _():
            for u in range(UNITS):
                mine = unit_lat(k, u) == lat

                @pl.when(jnp.logical_not(mine))
                def _():
                    pltpu.make_async_copy(st2.at[k, u], st2.at[k, u], r3s.at[k, u]).wait()

                @pl.when(mine)
                def _():
                    for d in range(1, nlat):
                        pltpu.make_async_copy(red.at[k, u], red.at[k, u], r4s.at[k, d]).wait()

            @pl.when(seg != k)
            def _():
                pltpu.make_async_copy(red.at[k], red.at[k], r5s.at[k]).wait()

        return carry

    lax.fori_loop(0, SECTIONS, ended, 0)
    last.wait_send()
    pltpu.make_async_copy(gw_ref.at[other], gw_ref.at[other], r6.at[1]).wait()


def per_device(nz, initial, kernel, bias, cotangent):
    y = lax.rem(lax.axis_index("segment"), 4)
    C, W = initial.shape[1], initial.shape[3]
    K3 = 3 * C
    lanes = -(-(K3 + 2) // 128) * 128
    half, part = K3 // 2, K3 // 4
    nlat = 2 * nz
    piece = half // PIECES
    unit = piece // UNITS

    stacked = jnp.concatenate([initial[None], cotangent[1:2], cotangent[0:1]], axis=0)
    rows = lax.dynamic_slice(
        stacked, (0, y, 0, 0, 0), (3, 1, C, 2, W)
    ).reshape(3, C, 2, W).transpose(2, 0, 1, 3)

    taps = kernel[0].reshape(C, 3, 3, C)
    taps = jnp.concatenate([taps[:, 0:1], taps[:, 2:3], taps[:, 1:2]], axis=1)
    flat = taps.transpose(2, 0, 1, 3).reshape(K3, K3)
    coarse = lax.reduce_precision(bias[0], 8, 7)
    fine = bias[0] - coarse
    pair = jnp.stack([coarse, fine], axis=1).astype(BF)
    side = jnp.pad(pair, ((C, C), (0, lanes - K3 - 2)))
    weights = jnp.concatenate([flat, side], axis=1)

    vm = pl.BlockSpec(memory_space=pltpu.VMEM)
    dma = pltpu.SemaphoreType.DMA
    so, sa, gw = pl.pallas_call(
        functools.partial(network_kernel, (C, W, nz)),
        out_shape=(
            jax.ShapeDtypeStruct((8, C, W), BF),
            jax.ShapeDtypeStruct((8, C, W), BF),
            jax.ShapeDtypeStruct((2, PIECES, UNITS, unit, lanes), BF),
        ),
        in_specs=[vm, vm],
        out_specs=(vm, vm, vm),
        scratch_shapes=[
            pltpu.VMEM((3, C, W), BF),
            pltpu.VMEM((SECTIONS, 2, 2, part, lanes), BF),
            pltpu.VMEM((3, K3, C), BF),
            pltpu.VMEM((APPS, lanes, W), BF),
            pltpu.VMEM((APPS + 1, K3, W), BF),
            pltpu.VMEM((APPS + 1, C, W), BF),
            pltpu.VMEM((SECTIONS, 2, PIECES, piece, lanes), BF),
            pltpu.VMEM((SECTIONS, PIECES, piece, lanes), BF),
            pltpu.VMEM((SECTIONS, PIECES, piece, lanes), BF),
            pltpu.VMEM((SECTIONS, 8, piece, lanes), BF),
            pltpu.VMEM((SECTIONS, UNITS, unit, lanes), BF),
            pltpu.VMEM((SECTIONS, nlat, unit, lanes), BF),
            pltpu.VMEM((SECTIONS, UNITS, unit, lanes), BF),
            dma((2, 4)),
            dma((19,)),
            dma((20,)),
            dma((2 * APPS, 2)),
            dma((2 * APPS, 2)),
            dma((2, SECTIONS)),
            dma((2, 8)),
            dma((SECTIONS,)),
            dma((SECTIONS,)),
            dma((SECTIONS, PIECES)),
            dma((SECTIONS, 8)),
            dma((SECTIONS, UNITS)),
            dma((SECTIONS, nlat)),
            dma((SECTIONS, nlat)),
            dma((SECTIONS, UNITS)),
            dma((SECTIONS,)),
            dma((PIECES,)),
            dma((2,)),
        ],
        compiler_params=pltpu.CompilerParams(
            collective_id=0, has_side_effects=True, vmem_limit_bytes=60 * 2**20
        ),
    )(rows, weights)

    def banded(slots):
        return slots.reshape(4, 2, C, W).transpose(0, 2, 1, 3)[None]

    normalizer = 1.0 / math.sqrt(initial.shape[0] * 2 * initial.shape[2] * nlat * W)
    grads = gw.reshape(K3, lanes).astype(F32) * normalizer
    core_grads = grads[:, :K3].reshape(3, C, 3, C).transpose(1, 2, 0, 3)
    core_grads = jnp.concatenate([core_grads[:, 0:1], core_grads[:, 2:3], core_grads[:, 1:2]], axis=1)
    return (
        banded(so),
        banded(sa).astype(F32),
        core_grads.reshape(1, C, 9, C),
        grads[C : 2 * C, K3][None],
    )


def solution(mesh):
    nz = mesh.shape["lat"] // 2
    return jax.shard_map(
        functools.partial(per_device, nz),
        mesh=mesh,
        in_specs=(
            P("dp", None, "lat", None),
            P("segment", None, None, None),
            P("segment", None),
            P(None, "dp", None, "lat", None),
        ),
        out_specs=(
            P("segment", "dp", None, "lat", None),
            P("segment", "dp", None, "lat", None),
            P("segment", None, None, None),
            P("segment", None),
        ),
        check_vma=False,
    )
```

```python
import functools
import math

import jax
import jax.numpy as jnp
from jax import lax
from jax.experimental import pallas as pl
from jax.experimental.pallas import tpu as pltpu
from jax.sharding import PartitionSpec as P

STEPS = 2
SECTIONS = 8
APPS = STEPS * SECTIONS
BF = jnp.bfloat16
F32 = jnp.float32
MESH = pl.DeviceIdType.MESH
HALO_UP, HALO_DN = 0, 1


def silu_value(values):
    return values / (1.0 + jnp.exp(-values))


def silu_slope(values):
    sigmoid_v = 1.0 / (1.0 + jnp.exp(-values))
    return sigmoid_v * (1.0 + values * (1.0 - sigmoid_v))


PIECES = 6
UNITS = 3


def network_kernel(
    dims, normalizer, x_ref, w_ref, b_ref, so_ref, sa_ref, kg_ref, bg_ref,
    gw_ref, xc, wall, b2, pbuf, gbuf, sbuf, dwf, cr, cs, r2, st2, r3, red, xsem, wss, wrs,
    hss, hrs, oss, ors, crs, crr, r2s, r2r, r3s, r3r, r4s, r4r, r5s, r5r, r6,
):
    C, W, nz = dims
    K3 = 3 * C
    half = K3 // 2
    part = half // 2
    lanes = pbuf.shape[1]
    nlat = 2 * nz
    nrow = 4 * nz
    piece = half // PIECES

    seg = lax.axis_index("segment")
    lat = lax.axis_index("lat")
    core = lax.axis_index("dp")
    x_lo, y = seg // 4, lax.rem(seg, 4)
    z, x_hi = lat // 2, lax.rem(lat, 2)
    x = 2 * x_hi + x_lo
    odd = lax.rem(z, 2)
    held = lax.rem(x_lo + x_hi, 2)
    band = 2 * z + lax.rem(x_hi + odd, 2)
    row = 2 * band + core
    has_up = row > 0
    has_dn = row < nrow - 1

    def at(px, py, pz, pc=core):
        return {"segment": lax.rem(px, 2) * 4 + py, "lat": pz * 2 + px // 2, "dp": pc}

    def holder(r):
        r_band = r // 2
        rz = r_band // 2
        hi = lax.rem(r_band + rz, 2)
        return {"segment": lax.rem(held + hi, 2) * 4 + y, "lat": rz * 2 + hi, "dp": lax.rem(r, 2)}

    up_dev = holder(jnp.maximum(row - 1, 0))
    dn_dev = holder(jnp.minimum(row + 1, nrow - 1))
    other = 1 - core
    partner = {"segment": seg, "lat": lat, "dp": other}
    y_up, y_dn = lax.rem(y + 1, 4), lax.rem(y + 3, 4)
    x_up, x_dn = lax.rem(x + 1, 4), lax.rem(x + 3, 4)

    barrier = pltpu.get_barrier_semaphore()
    for d in range(1, 32):
        dx, dy, dc = d // 8, (d // 2) % 4, d % 2
        peer = at(lax.rem(x + dx, 4), lax.rem(y + dy, 4), z, lax.rem(core + dc, 2))
        pl.semaphore_signal(barrier, inc=1, device_id=peer, device_id_type=MESH)
    for d in range(1, nz):
        for hi in range(2):
            peer = {"segment": seg, "lat": lax.rem(z + d, nz) * 2 + hi, "dp": core}
            pl.semaphore_signal(barrier, inc=1, device_id=peer, device_id_type=MESH)
    for d in (1, nz - 1):
        peer = {"segment": seg, "lat": lax.rem(z + d, nz) * 2 + x_hi, "dp": other}
        pl.semaphore_signal(barrier, inc=1, device_id=peer, device_id_type=MESH)
    pl.semaphore_wait(barrier, 31 + 2 * (nz - 1) + 2)

    def remote(src, dst, ssem, rsem, dev):
        return pltpu.make_async_remote_copy(
            src_ref=src, dst_ref=dst, send_sem=ssem, recv_sem=rsem, device_id=dev, device_id_type=MESH
        )

    giver = core == held
    stays = jnp.logical_and(giver, odd == 0)
    home_x = x + odd * (3 - 2 * x)

    def given(r, what):
        span = pl.ds(0, 1) if what == 0 else pl.ds(1, 2)
        return remote(
            x_ref.at[r, span], xc.at[span], xsem.at[0, 2 * r + what], xsem.at[1, what], at(home_x, y, z, r)
        )

    def leaves(r):
        return jnp.logical_and(giver, jnp.logical_or(odd == 1, core != r))

    for what in range(2):
        for r in range(2):
            @pl.when(leaves(r))
            def _():
                given(r, what).start()

    @pl.when(stays)
    def _():
        xc[...] = x_ref[core]

    def rows_wait(what):
        span = pl.ds(0, 1) if what == 0 else pl.ds(1, 2)

        @pl.when(jnp.logical_not(stays))
        def _():
            pltpu.make_async_copy(xc.at[span], xc.at[span], xsem.at[1, what]).wait()

    lane = lax.broadcasted_iota(jnp.int32, (C, lanes - K3), 1)
    offsets = b_ref[:, 0 : lanes - K3]
    coarse = offsets.astype(BF).astype(F32)
    side = jnp.where(lane == 0, coarse, jnp.where(lane == 1, offsets - coarse, 0.0)).astype(BF)
    table = [
        jnp.concatenate(
            [w_ref[q], w_ref[6 + q], w_ref[3 + q], side if q == 1 else jnp.zeros_like(side)], axis=1
        )
        for q in range(3)
    ]
    wall[seg] = jnp.concatenate(table, axis=0).reshape(2, 2, part, lanes)
    sec_dn, sec_up = x_lo * 4 + y_dn, x_lo * 4 + y_up
    sec_far = x_lo * 4 + lax.rem(y + 2, 4)
    sends = []

    def go(copy):
        copy.start()
        sends.append(copy)

    def send_w(index, src, slot, dev):
        go(remote(src, src, wss.at[index], wrs.at[slot], dev))

    dev_yu, dev_yd = at(x, y_up, z), at(x, y_dn, z)
    dev_xu, dev_xd = at(x_up, y, z), at(x_dn, y, z)
    send_w(0, wall.at[seg, core], 0, dev_yu)
    send_w(1, wall.at[seg, core], 1, dev_yd)
    send_w(2, wall.at[seg, core, 0], 4 + 2 * y, dev_xu)
    send_w(3, wall.at[seg, core, 1], 5 + 2 * y, dev_xd)

    def landed(ref, slot):
        pltpu.make_async_copy(ref, ref, wrs.at[slot]).wait()

    def spread(index, sec, sy):
        send_w(index, wall.at[sec, core, 0], 4 + 2 * sy, dev_xu)
        send_w(index + 1, wall.at[sec, core, 1], 5 + 2 * sy, dev_xd)
        send_w(index + 2, wall.at[sec, core], 12 + sec, partner)

    landed(wall.at[sec_dn, core], 0)
    send_w(4, wall.at[sec_dn, core, 0], 2, dev_yu)
    spread(5, sec_dn, y_dn)
    landed(wall.at[sec_up, core], 1)
    send_w(8, wall.at[sec_up, core, 1], 3, dev_yd)
    spread(9, sec_up, y_up)
    landed(wall.at[sec_far, core, 0], 2)
    landed(wall.at[sec_far, core, 1], 3)
    spread(12, sec_far, lax.rem(y + 2, 4))
    for j in range(4):
        sy = lax.rem(y + j, 4)
        sec = (1 - x_lo) * 4 + sy
        landed(wall.at[sec, core, 0], 4 + 2 * sy)
        landed(wall.at[sec, core, 1], 5 + 2 * sy)
        send_w(15 + j, wall.at[sec, core], 12 + sec, partner)
    for j in range(1, 8):
        sec = lax.rem(seg + j, 8)
        landed(wall.at[sec, other], 12 + sec)

    ones = (lax.broadcasted_iota(jnp.int32, (lanes - K3, W), 0) < 2).astype(F32).astype(BF)

    @pl.loop(0, APPS)
    def _(a):
        pbuf[a, K3:, :] = ones

    @pl.when(jnp.logical_not(has_up))
    def _():
        @pl.loop(0, APPS)
        def _(a):
            pbuf[a, 0:C, :] = jnp.zeros((C, W), BF)
            gbuf[a + 1, 0:C, :] = jnp.zeros((C, W), BF)

    @pl.when(jnp.logical_not(has_dn))
    def _():
        @pl.loop(0, APPS)
        def _(a):
            pbuf[a, C : 2 * C, :] = jnp.zeros((C, W), BF)
            gbuf[a + 1, C : 2 * C, :] = jnp.zeros((C, W), BF)

    rows_wait(0)
    sbuf[0] = xc[0]

    def halo_copies(buf, slot, step):
        own = buf.at[slot, pl.ds(2 * C, C), :]
        to_up = remote(own, buf.at[slot, pl.ds(C, C), :], hss.at[step, 0], hrs.at[step, 1], up_dev)
        to_dn = remote(own, buf.at[slot, pl.ds(0, C), :], hss.at[step, 1], hrs.at[step, 0], dn_dev)
        return to_up, to_dn

    def halo_start(buf, slot, step):
        to_up, to_dn = halo_copies(buf, slot, step)

        @pl.when(has_up)
        def _():
            to_up.start()

        @pl.when(has_dn)
        def _():
            to_dn.start()

    def halo_wait(buf, slot, step):
        to_up, to_dn = halo_copies(buf, slot, step)

        @pl.when(has_up)
        def _():
            to_up.wait_send()
            pltpu.make_async_copy(buf.at[slot, pl.ds(0, C), :], buf.at[slot, pl.ds(0, C), :], hrs.at[step, 0]).wait()

        @pl.when(has_dn)
        def _():
            to_dn.wait_send()
            pltpu.make_async_copy(buf.at[slot, pl.ds(C, C), :], buf.at[slot, pl.ds(C, C), :], hrs.at[step, 1]).wait()

    out_slot = y * 2 + core

    def out_copy(src, dst, which, k):
        dev = {"segment": k, "lat": band, "dp": held}
        return remote(src, dst.at[out_slot], oss.at[which, k], ors.at[which, out_slot], dev)

    def is_self(k):
        return jnp.logical_and(seg == k, stays)

    def out_send(src, dst, which, k):
        mine = is_self(k)

        @pl.when(mine)
        def _():
            dst[out_slot] = src[...]

        @pl.when(jnp.logical_not(mine))
        def _():
            out_copy(src, dst, which, k).start()

    def shifted_sum(parts, sign):
        minus, same, plus = parts[0:C], parts[C : 2 * C], parts[2 * C :]
        return same + pltpu.roll(minus, 1 if sign < 0 else W - 1, 1) + pltpu.roll(plus, W - 1 if sign < 0 else 1, 1)

    def forward(a, carry):
        k = lax.rem(a, SECTIONS)
        state = sbuf[a].astype(F32)
        pbuf[a, 2 * C : K3, :] = silu_value(state).astype(BF)
        halo_start(pbuf, a, a)
        own = jnp.dot(
            wall[k, :, :, :, 2 * C :].reshape(K3, lanes - 2 * C), pbuf[a, 2 * C :, :], preferred_element_type=F32
        )
        halo_wait(pbuf, a, a)
        rest = jnp.dot(
            wall[k, :, :, :, 0 : 2 * C].reshape(K3, 2 * C), pbuf[a, 0 : 2 * C, :], preferred_element_type=F32
        )
        sbuf[a + 1] = (state + shifted_sum(own + rest, -1)).astype(BF)

        @pl.when(a >= APPS - SECTIONS)
        def _():
            out_send(sbuf.at[a + 1], so_ref, 0, k)

        return carry

    lax.fori_loop(0, APPS, forward, 0)

    rows_wait(1)
    gbuf[APPS, 2 * C :, :] = xc[1]

    def turned_weights(k):
        for q in range(3):
            flat = wall[k].reshape(K3, lanes)[q * C : (q + 1) * C]
            turned = flat[:, : K3].T
            b2[1, q * C : (q + 1) * C, :] = turned[0:C]
            b2[0, q * C : (q + 1) * C, :] = turned[C : 2 * C]
            b2[2, q * C : (q + 1) * C, :] = turned[2 * C :]

    def tapped(grad):
        wide = grad.astype(F32)
        return jnp.concatenate(
            [pltpu.roll(wide, W - 1, 1).astype(BF), grad, pltpu.roll(wide, 1, 1).astype(BF)], axis=0
        )

    def pair_and_scatter(k):
        pltpu.make_async_copy(cr.at[k], cr.at[k], crr.at[k]).wait()
        for jx in range(2):
            for jy in range(3):
                j = 3 * jx + jy
                cs[k, j] = (dwf[k, core, j].astype(F32) + cr[k, j].astype(F32)).astype(BF)
                near = x_lo == jx
                far_x = lax.rem(x + (1 if jy % 2 == 0 else 3), 4)
                home = at(jnp.where(near, x, far_x), jy, z)
                slot = jnp.where(near, y, 4 + y)
                mine = jnp.logical_and(near, y == jy)

                @pl.when(mine)
                def _():
                    r2[k, slot] = cs[k, j]

                @pl.when(jnp.logical_not(mine))
                def _():
                    remote(cs.at[k, j], r2.at[k, slot], r2s.at[k, j], r2r.at[k, slot], home).start()

    def unit_lat(k, u):
        return lax.rem((nlat // 3) * u + 2 * k, nlat)

    def sum_and_scatter(k):
        @pl.when(y < 3)
        def _():
            total = r2[k, y].astype(F32)
            for d in range(1, 4):
                src = lax.rem(y + d, 4)
                pltpu.make_async_copy(r2.at[k, src], r2.at[k, src], r2r.at[k, src]).wait()
                total = total + r2[k, src].astype(F32)
            for src in range(4, 8):
                pltpu.make_async_copy(r2.at[k, src], r2.at[k, src], r2r.at[k, src]).wait()
                total = total + r2[k, src].astype(F32)
            st2[k] = total.astype(BF).reshape(UNITS, piece // UNITS, lanes)
            for u in range(UNITS):
                goal = unit_lat(k, u)

                @pl.when(goal != lat)
                def _():
                    dev = {"segment": seg, "lat": goal, "dp": core}
                    remote(st2.at[k, u], r3.at[k, lat], r3s.at[k, u], r3r.at[k, lat], dev).start()

    def lat_sum(k):
        for u in range(UNITS):
            @pl.when(jnp.logical_and(y < 3, unit_lat(k, u) == lat))
            def _():
                unit = st2[k, u].astype(F32)
                for d in range(1, nlat):
                    src = lax.rem(lat + d, nlat)
                    pltpu.make_async_copy(r3.at[k, src], r3.at[k, src], r3r.at[k, src]).wait()
                    unit = unit + r3[k, src].astype(F32)
                red[k, u] = unit.astype(BF)
                for d in range(1, nlat):
                    dev = {"segment": seg, "lat": lax.rem(lat + d, nlat), "dp": core}
                    remote(red.at[k, u], red.at[k, u], r4s.at[k, d], r4r.at[k, u], dev).start()

    my_piece = 3 * x_lo + jnp.minimum(y, 2)

    def deliver(k):
        @pl.when(y < 3)
        def _():
            for u in range(UNITS):
                @pl.when(unit_lat(k, u) != lat)
                def _():
                    pltpu.make_async_copy(red.at[k, u], red.at[k, u], r4r.at[k, u]).wait()

            @pl.when(seg == k)
            def _():
                gw_ref[core, my_piece] = red[k]

            @pl.when(seg != k)
            def _():
                dev = {"segment": k, "lat": lat, "dp": core}
                remote(red.at[k], gw_ref.at[core, my_piece], r5s.at[k], r5r.at[my_piece], dev).start()

    def staged(a):
        for lag, stage in ((1, pair_and_scatter), (3, sum_and_scatter), (5, lat_sum), (7, deliver)):
            k = a + lag

            @pl.when(jnp.logical_and(k >= 0, k < SECTIONS))
            def _():
                stage(k)

    def backward(a, with_weights):
        k = lax.rem(a, SECTIONS)
        step = APPS + APPS - 1 - a
        slot = a + 1
        halo_start(gbuf, slot, step)
        grad = gbuf[slot, 2 * C :, :]
        turned_weights(k)
        own = jnp.dot(b2[2], grad, preferred_element_type=F32)
        if with_weights:
            later = a + SECTIONS
            taps = jnp.concatenate([tapped(grad), tapped(gbuf[later + 1, 2 * C :, :])], axis=1)
            acts = jnp.concatenate([pbuf[a], pbuf[later]], axis=1)
            dw = lax.dot_general(taps, acts, (((1,), (1,)), ((), ())), preferred_element_type=F32)
            dwf[k] = dw.astype(BF).reshape(2, PIECES, piece, lanes)
            remote(dwf.at[k, other], cr.at[k], crs.at[k], crr.at[k], partner).start()
            staged(a)

        halo_wait(gbuf, slot, step)
        rest = jnp.dot(b2[0], gbuf[slot, 0:C, :], preferred_element_type=F32) + jnp.dot(
            b2[1], gbuf[slot, C : 2 * C, :], preferred_element_type=F32
        )
        slope = silu_slope(sbuf[a].astype(F32))
        adjoint = grad.astype(F32) + slope * shifted_sum(own + rest, 1)
        if not with_weights:
            adjoint = adjoint + jnp.where(a == SECTIONS, xc[2].astype(F32), 0.0)
        gbuf[a, 2 * C :, :] = adjoint.astype(BF)
        if with_weights:
            out_send(gbuf.at[a, pl.ds(2 * C, C), :], sa_ref, 1, k)

    def backward_late(i, carry):
        backward(APPS - 1 - i, False)
        return carry

    def backward_early(i, carry):
        backward(SECTIONS - 1 - i, True)
        return carry

    lax.fori_loop(0, SECTIONS, backward_late, 0)
    lax.fori_loop(0, SECTIONS, backward_early, 0)

    def drain(i, carry):
        staged(-1 - i)
        return carry

    lax.fori_loop(0, 7, drain, 0)
    for j in range(PIECES):
        @pl.when(seg != (j // 3) * 4 + j % 3)
        def _():
            pltpu.make_async_copy(gw_ref.at[core, j], gw_ref.at[core, j], r5r.at[j]).wait()
    last = remote(gw_ref.at[core], gw_ref.at[core], r6.at[0], r6.at[1], partner)
    last.start()

    for copy in sends:
        copy.wait_send()
    for k in range(SECTIONS):
        for which, (dst, src) in enumerate(
            ((so_ref, sbuf.at[APPS - SECTIONS + k + 1]), (sa_ref, gbuf.at[k, pl.ds(2 * C, C), :]))
        ):
            @pl.when(jnp.logical_not(is_self(k)))
            def _():
                out_copy(src, dst, which, k).wait_send()

    for what in range(2):
        for r in range(2):
            @pl.when(leaves(r))
            def _():
                given(r, what).wait_send()

    for s in range(8):
        from_self = jnp.logical_and(stays, jnp.logical_and(core == s % 2, y == s // 2))
        for which, dst in enumerate((so_ref, sa_ref)):
            @pl.when(jnp.logical_not(from_self))
            def _():
                pltpu.make_async_copy(dst.at[s], dst.at[s], ors.at[which, s]).wait()

    def ended(k, carry):
        pltpu.make_async_copy(dwf.at[k, other], dwf.at[k, other], crs.at[k]).wait()
        for j in range(PIECES):
            @pl.when(seg != (j // 3) * 4 + j % 3)
            def _():
                pltpu.make_async_copy(cs.at[k, j], cs.at[k, j], r2s.at[k, j]).wait()

        @pl.when(y < 3)
        def _():
            for u in range(UNITS):
                mine = unit_lat(k, u) == lat

                @pl.when(jnp.logical_not(mine))
                def _():
                    pltpu.make_async_copy(st2.at[k, u], st2.at[k, u], r3s.at[k, u]).wait()

                @pl.when(mine)
                def _():
                    for d in range(1, nlat):
                        pltpu.make_async_copy(red.at[k, u], red.at[k, u], r4s.at[k, d]).wait()

            @pl.when(seg != k)
            def _():
                pltpu.make_async_copy(red.at[k], red.at[k], r5s.at[k]).wait()

        return carry

    lax.fori_loop(0, SECTIONS, ended, 0)
    last.wait_send()
    pltpu.make_async_copy(gw_ref.at[other], gw_ref.at[other], r6.at[1]).wait()
    grads = gw_ref[...].reshape(K3, lanes).astype(F32) * normalizer
    for q in range(3):
        block = grads[q * C : (q + 1) * C]
        kg_ref[q] = block[:, 0:C]
        kg_ref[6 + q] = block[:, C : 2 * C]
        kg_ref[3 + q] = block[:, 2 * C : K3]
        if q == 1:
            bg_ref[...] = block[:, lanes - 128 :].T[K3 - lanes + 128 : K3 - lanes + 129]


def per_device(nz, initial, kernel, bias, cotangent):
    y = lax.rem(lax.axis_index("segment"), 4)
    C, W = initial.shape[1], initial.shape[3]
    K3 = 3 * C
    lanes = -(-(K3 + 2) // 128) * 128
    half, part = K3 // 2, K3 // 4
    nlat = 2 * nz
    piece = half // PIECES
    unit = piece // UNITS

    normalizer = 1.0 / math.sqrt(initial.shape[0] * 2 * initial.shape[2] * nlat * W)
    rows = jnp.stack([
        lax.dynamic_index_in_dim(band, y, 0, keepdims=False)
        for band in (initial, cotangent[1], cotangent[0])
    ]).transpose(2, 0, 1, 3)
    weights = kernel[0].transpose(1, 0, 2)
    offsets = jnp.broadcast_to(bias[0][:, None], (C, 128))

    vm = pl.BlockSpec(memory_space=pltpu.VMEM)
    dma = pltpu.SemaphoreType.DMA
    so, sa, kg, bg = pl.pallas_call(
        functools.partial(network_kernel, (C, W, nz), normalizer),
        out_shape=(
            jax.ShapeDtypeStruct((8, C, W), BF),
            jax.ShapeDtypeStruct((8, C, W), BF),
            jax.ShapeDtypeStruct((9, C, C), F32),
            jax.ShapeDtypeStruct((1, C), F32),
        ),
        in_specs=[vm, vm, vm],
        out_specs=(vm, vm, vm, vm),
        scratch_shapes=[
            pltpu.VMEM((2, PIECES, UNITS, unit, lanes), BF),
            pltpu.VMEM((3, C, W), BF),
            pltpu.VMEM((SECTIONS, 2, 2, part, lanes), BF),
            pltpu.VMEM((3, K3, C), BF),
            pltpu.VMEM((APPS, lanes, W), BF),
            pltpu.VMEM((APPS + 1, K3, W), BF),
            pltpu.VMEM((APPS + 1, C, W), BF),
            pltpu.VMEM((SECTIONS, 2, PIECES, piece, lanes), BF),
            pltpu.VMEM((SECTIONS, PIECES, piece, lanes), BF),
            pltpu.VMEM((SECTIONS, PIECES, piece, lanes), BF),
            pltpu.VMEM((SECTIONS, 8, piece, lanes), BF),
            pltpu.VMEM((SECTIONS, UNITS, unit, lanes), BF),
            pltpu.VMEM((SECTIONS, nlat, unit, lanes), BF),
            pltpu.VMEM((SECTIONS, UNITS, unit, lanes), BF),
            dma((2, 4)),
            dma((19,)),
            dma((20,)),
            dma((2 * APPS, 2)),
            dma((2 * APPS, 2)),
            dma((2, SECTIONS)),
            dma((2, 8)),
            dma((SECTIONS,)),
            dma((SECTIONS,)),
            dma((SECTIONS, PIECES)),
            dma((SECTIONS, 8)),
            dma((SECTIONS, UNITS)),
            dma((SECTIONS, nlat)),
            dma((SECTIONS, nlat)),
            dma((SECTIONS, UNITS)),
            dma((SECTIONS,)),
            dma((PIECES,)),
            dma((2,)),
        ],
        compiler_params=pltpu.CompilerParams(
            collective_id=0, has_side_effects=True, vmem_limit_bytes=60 * 2**20
        ),
    )(rows, weights, offsets)

    def banded(slots):
        return slots.reshape(4, 2, C, W).transpose(0, 2, 1, 3)[None]

    return (
        banded(so),
        banded(sa).astype(F32),
        kg.transpose(1, 0, 2)[None],
        bg,
    )


def solution(mesh):
    nz = mesh.shape["lat"] // 2
    return jax.shard_map(
        functools.partial(per_device, nz),
        mesh=mesh,
        in_specs=(
            P("dp", None, "lat", None),
            P("segment", None, None, None),
            P("segment", None),
            P(None, "dp", None, "lat", None),
        ),
        out_specs=(
            P("segment", "dp", None, "lat", None),
            P("segment", "dp", None, "lat", None),
            P("segment", None, None, None),
            P("segment", None),
        ),
        check_vma=False,
    )
```

```python
import functools
import math

import jax
import jax.numpy as jnp
from jax import lax
from jax.experimental import pallas as pl
from jax.experimental.pallas import tpu as pltpu
from jax.sharding import PartitionSpec as P

STEPS = 2
SECTIONS = 8
APPS = STEPS * SECTIONS
BF = jnp.bfloat16
F32 = jnp.float32
MESH = pl.DeviceIdType.MESH
REACH = (1, -1, 2, -2)


def silu_value(values):
    return values / (1.0 + jnp.exp(-values))


def silu_slope(values):
    sigmoid_v = 1.0 / (1.0 + jnp.exp(-values))
    return sigmoid_v * (1.0 + values * (1.0 - sigmoid_v))


PIECES = 6
UNITS = 3


def network_kernel(
    dims, normalizer, x_ref, w_ref, b_ref, so_ref, sa_ref, kg_ref, bg_ref,
    gw_ref, xc, wall, b2, pbuf, gbuf, sbuf, dwf, cr, cs, r2, st2, r3, red, xsem, wss, wrs,
    hss, hrs, oss, ors, crs, crr, r2s, r2r, r3s, r3r, r4s, r4r, r5s, r5r, r6,
):
    C, W, nz = dims
    K3 = 3 * C
    half = K3 // 2
    part = half // 2
    lanes = pbuf.shape[1]
    nlat = 2 * nz
    nrow = 4 * nz
    piece = half // PIECES

    seg = lax.axis_index("segment")
    lat = lax.axis_index("lat")
    core = lax.axis_index("dp")
    x_lo, y = seg // 4, lax.rem(seg, 4)
    z, x_hi = lat // 2, lax.rem(lat, 2)
    x = 2 * x_hi + x_lo
    odd = lax.rem(z, 2)
    held = lax.rem(x_lo + x_hi, 2)
    band = 2 * z + lax.rem(x_hi + odd, 2)
    row = 2 * band + core
    has_up = row > 0
    has_dn = row < nrow - 1

    def at(px, py, pz, pc=core):
        return {"segment": lax.rem(px, 2) * 4 + py, "lat": pz * 2 + px // 2, "dp": pc}

    def holder(r):
        r_band = r // 2
        rz = r_band // 2
        hi = lax.rem(r_band + rz, 2)
        return {"segment": lax.rem(held + hi, 2) * 4 + y, "lat": rz * 2 + hi, "dp": lax.rem(r, 2)}

    def inside(shift):
        return jnp.logical_and(row + shift >= 0, row + shift < nrow)

    other = 1 - core
    partner = {"segment": seg, "lat": lat, "dp": other}
    y_up, y_dn = lax.rem(y + 1, 4), lax.rem(y + 3, 4)
    x_up, x_dn = lax.rem(x + 1, 4), lax.rem(x + 3, 4)

    barrier = pltpu.get_barrier_semaphore()
    for d in range(1, 32):
        dx, dy, dc = d // 8, (d // 2) % 4, d % 2
        peer = at(lax.rem(x + dx, 4), lax.rem(y + dy, 4), z, lax.rem(core + dc, 2))
        pl.semaphore_signal(barrier, inc=1, device_id=peer, device_id_type=MESH)
    for d in range(1, nz):
        for hi in range(2):
            peer = {"segment": seg, "lat": lax.rem(z + d, nz) * 2 + hi, "dp": core}
            pl.semaphore_signal(barrier, inc=1, device_id=peer, device_id_type=MESH)
    for d in (1, nz - 1):
        peer = {"segment": seg, "lat": lax.rem(z + d, nz) * 2 + x_hi, "dp": other}
        pl.semaphore_signal(barrier, inc=1, device_id=peer, device_id_type=MESH)
    ones = (lax.broadcasted_iota(jnp.int32, (lanes - K3, W), 0) < 2).astype(F32).astype(BF)
    for shift in REACH:
        @pl.when(jnp.logical_not(inside(shift)))
        def _():
            @pl.loop(0, APPS // 2)
            def _(t):
                sbuf[2 * t, 2 + shift] = jnp.zeros((C, W), BF)
                gbuf[2 * t + 2, 2 + shift] = jnp.zeros((C, W), BF)

    lane = lax.broadcasted_iota(jnp.int32, (C, lanes - K3), 1)
    offsets = b_ref[:, 0 : lanes - K3]
    coarse = offsets.astype(BF).astype(F32)
    side = jnp.where(lane == 0, coarse, jnp.where(lane == 1, offsets - coarse, 0.0)).astype(BF)
    table = [
        jnp.concatenate(
            [w_ref[q], w_ref[6 + q], w_ref[3 + q], side if q == 1 else jnp.zeros_like(side)], axis=1
        )
        for q in range(3)
    ]
    wall[seg] = jnp.concatenate(table, axis=0).reshape(2, 2, part, lanes)
    pl.semaphore_wait(barrier, 31 + 2 * (nz - 1) + 2)

    def remote(src, dst, ssem, rsem, dev):
        return pltpu.make_async_remote_copy(
            src_ref=src, dst_ref=dst, send_sem=ssem, recv_sem=rsem, device_id=dev, device_id_type=MESH
        )

    giver = core == held
    stays = jnp.logical_and(giver, odd == 0)
    home_x = x + odd * (3 - 2 * x)

    def given(r, what):
        span = pl.ds(0, 1) if what == 0 else pl.ds(1, 2)
        return remote(
            x_ref.at[r, span], xc.at[span], xsem.at[0, 2 * r + what], xsem.at[1, what], at(home_x, y, z, r)
        )

    def leaves(r):
        return jnp.logical_and(giver, jnp.logical_or(odd == 1, core != r))

    for what in range(2):
        for r in range(2):
            @pl.when(leaves(r))
            def _():
                given(r, what).start()

    @pl.when(stays)
    def _():
        xc[...] = x_ref[core]

    def rows_wait(what):
        span = pl.ds(0, 1) if what == 0 else pl.ds(1, 2)

        @pl.when(jnp.logical_not(stays))
        def _():
            pltpu.make_async_copy(xc.at[span], xc.at[span], xsem.at[1, what]).wait()

    sec_dn, sec_up = x_lo * 4 + y_dn, x_lo * 4 + y_up
    sec_far = x_lo * 4 + lax.rem(y + 2, 4)
    sends = []

    def go(copy):
        copy.start()
        sends.append(copy)

    def send_w(index, src, slot, dev):
        go(remote(src, src, wss.at[index], wrs.at[slot], dev))

    dev_yu, dev_yd = at(x, y_up, z), at(x, y_dn, z)
    dev_xu, dev_xd = at(x_up, y, z), at(x_dn, y, z)
    send_w(0, wall.at[seg, core, 0], 0, dev_yu)
    send_w(1, wall.at[seg, core, 1], 1, dev_yd)
    send_w(2, wall.at[seg, core, 0], 4 + 2 * y, dev_xu)
    send_w(3, wall.at[seg, core, 1], 5 + 2 * y, dev_xd)
    send_w(19, wall.at[seg, core, 1], 20, dev_yu)
    send_w(20, wall.at[seg, core, 0], 21, dev_yd)

    def landed(ref, slot):
        pltpu.make_async_copy(ref, ref, wrs.at[slot]).wait()

    def across(index, sec, part_at):
        slot = 4 + 2 * lax.rem(sec, 4) + part_at
        send_w(index, wall.at[sec, core, part_at], slot, dev_xu if part_at == 0 else dev_xd)

    def beside(index, sec):
        send_w(index, wall.at[sec, core], 12 + sec, partner)

    landed(wall.at[sec_dn, core, 0], 0)
    send_w(4, wall.at[sec_dn, core, 0], 2, dev_yu)
    across(5, sec_dn, 0)
    landed(wall.at[sec_up, core, 1], 1)
    send_w(8, wall.at[sec_up, core, 1], 3, dev_yd)
    across(10, sec_up, 1)
    landed(wall.at[sec_dn, core, 1], 20)
    across(6, sec_dn, 1)
    beside(7, sec_dn)
    landed(wall.at[sec_up, core, 0], 21)
    across(9, sec_up, 0)
    beside(11, sec_up)
    landed(wall.at[sec_far, core, 0], 2)
    across(12, sec_far, 0)
    landed(wall.at[sec_far, core, 1], 3)
    across(13, sec_far, 1)
    beside(14, sec_far)

    def beside_copy(sec):
        half_ref = wall.at[sec, core]
        return remote(half_ref, half_ref, wss.at[15 + lax.rem(sec, 4)], wrs.at[12 + sec], partner)

    def take_section(sec):
        @pl.when(jnp.logical_and(sec < SECTIONS, sec // 4 != x_lo))
        def _():
            sy = lax.rem(sec, 4)
            landed(wall.at[sec, core, 0], 4 + 2 * sy)
            landed(wall.at[sec, core, 1], 5 + 2 * sy)
            beside_copy(sec).start()

    def need_section(sec):
        @pl.when(jnp.logical_and(sec < SECTIONS, sec != seg))
        def _():
            landed(wall.at[sec, other], 12 + sec)

    take_section(jnp.int32(0))
    take_section(jnp.int32(1))
    rows_wait(0)
    sbuf[0, 2] = xc[0]

    def halo_copy(buf, slot, step, shift):
        return remote(
            buf.at[slot, 2], buf.at[slot, 2 - shift], hss.at[step, 2 + shift], hrs.at[step, 2 - shift],
            holder(jnp.clip(row + shift, 0, nrow - 1)),
        )

    def halo_start(buf, slot, step):
        for shift in REACH:
            @pl.when(inside(shift))
            def _():
                halo_copy(buf, slot, step, shift).start()

    def halo_wait(buf, slot, step):
        for shift in REACH:
            @pl.when(inside(shift))
            def _():
                there = buf.at[slot, 2 + shift]
                pltpu.make_async_copy(there, there, hrs.at[step, 2 + shift]).wait()

        for shift in REACH:
            @pl.when(inside(shift))
            def _():
                halo_copy(buf, slot, step, shift).wait_send()

    out_slot = y * 2 + core

    def out_copy(src, dst, which, k):
        dev = {"segment": k, "lat": band, "dp": held}
        return remote(src, dst.at[out_slot], oss.at[which, k], ors.at[which, out_slot], dev)

    def is_self(k):
        return jnp.logical_and(seg == k, stays)

    def out_send(src, dst, which, k):
        mine = is_self(k)

        @pl.when(mine)
        def _():
            dst[out_slot] = src[...]

        @pl.when(jnp.logical_not(mine))
        def _():
            out_copy(src, dst, which, k).start()

    def shifted_sum(parts, sign):
        minus, same, plus = parts[0:C], parts[C : 2 * C], parts[2 * C :]
        return same + pltpu.roll(minus, 1 if sign < 0 else W - 1, 1) + pltpu.roll(plus, W - 1 if sign < 0 else 1, 1)

    def kept(shift, values):
        return jnp.where(inside(shift), values, jnp.zeros_like(values))

    def beside_each_other(*blocks):
        return jnp.concatenate(blocks, axis=1)

    def activated(state):
        return silu_value(state.astype(F32)).astype(BF)

    def state_out(number):
        @pl.when(number > APPS - SECTIONS)
        def _():
            out_send(sbuf.at[number, 2], so_ref, 0, number - 1 - (APPS - SECTIONS))

    def forward(t, carry):
        a = 2 * t
        halo_start(sbuf, a, t)
        take_section(a + 2)
        take_section(a + 3)
        state_out(a - 1)
        state_out(a)
        need_section(a)
        need_section(a + 1)
        k = lax.rem(a, SECTIONS)
        table = wall[k].reshape(K3, lanes)
        halo_wait(sbuf, a, t)
        acts = [activated(sbuf[a, i]) for i in range(5)]
        pbuf[a] = jnp.concatenate([acts[1], acts[3], acts[2], ones], axis=0)
        wide = jnp.concatenate(
            [
                beside_each_other(acts[0], acts[1], acts[2]),
                beside_each_other(acts[2], acts[3], acts[4]),
                beside_each_other(acts[1], acts[2], acts[3]),
                beside_each_other(ones, ones, ones),
            ],
            axis=0,
        )
        sums = jnp.dot(table, wide, preferred_element_type=F32)
        nexts = []
        for m in range(3):
            branch = shifted_sum(sums[:, m * W : (m + 1) * W], -1)
            value = kept(m - 1, (sbuf[a, 1 + m].astype(F32) + branch).astype(BF))
            sbuf[a + 1, 1 + m] = value
            nexts.append(value)
        acts = [activated(value) for value in nexts]
        column = jnp.concatenate([acts[0], acts[2], acts[1], ones], axis=0)
        pbuf[a + 1] = column
        sums = jnp.dot(wall[lax.rem(a + 1, SECTIONS)].reshape(K3, lanes), column, preferred_element_type=F32)
        sbuf[a + 2, 2] = (nexts[1].astype(F32) + shifted_sum(sums, -1)).astype(BF)
        return carry

    lax.fori_loop(0, APPS // 2, forward, 0)

    rows_wait(1)
    gbuf[APPS, 2] = xc[1]

    def turned_weights(k, which):
        table = wall[k].reshape(K3, lanes)
        for q in range(3):
            turned = table[q * C : (q + 1) * C, :K3].T
            b2[which, 1, q * C : (q + 1) * C, :] = turned[0:C]
            b2[which, 0, q * C : (q + 1) * C, :] = turned[C : 2 * C]
            b2[which, 2, q * C : (q + 1) * C, :] = turned[2 * C :]

    def tapped(grad):
        wide = grad.astype(F32)
        return jnp.concatenate(
            [pltpu.roll(wide, W - 1, 1).astype(BF), grad, pltpu.roll(wide, 1, 1).astype(BF)], axis=0
        )

    def pair_and_scatter(k):
        pltpu.make_async_copy(cr.at[k], cr.at[k], crr.at[k]).wait()
        for jx in range(2):
            for jy in range(3):
                j = 3 * jx + jy
                cs[k, j] = (dwf[k, core, j].astype(F32) + cr[k, j].astype(F32)).astype(BF)
                near = x_lo == jx
                far_x = lax.rem(x + (1 if jy % 2 == 0 else 3), 4)
                home = at(jnp.where(near, x, far_x), jy, z)
                slot = jnp.where(near, y, 4 + y)
                mine = jnp.logical_and(near, y == jy)

                @pl.when(mine)
                def _():
                    r2[k, slot] = cs[k, j]

                @pl.when(jnp.logical_not(mine))
                def _():
                    remote(cs.at[k, j], r2.at[k, slot], r2s.at[k, j], r2r.at[k, slot], home).start()

    def unit_lat(k, u):
        return lax.rem((nlat // 3) * u + 2 * k, nlat)

    def sum_and_scatter(k):
        @pl.when(y < 3)
        def _():
            total = r2[k, y].astype(F32)
            for d in range(1, 4):
                src = lax.rem(y + d, 4)
                pltpu.make_async_copy(r2.at[k, src], r2.at[k, src], r2r.at[k, src]).wait()
                total = total + r2[k, src].astype(F32)
            for src in range(4, 8):
                pltpu.make_async_copy(r2.at[k, src], r2.at[k, src], r2r.at[k, src]).wait()
                total = total + r2[k, src].astype(F32)
            st2[k] = total.astype(BF).reshape(UNITS, piece // UNITS, lanes)
            for u in range(UNITS):
                goal = unit_lat(k, u)

                @pl.when(goal != lat)
                def _():
                    dev = {"segment": seg, "lat": goal, "dp": core}
                    remote(st2.at[k, u], r3.at[k, lat], r3s.at[k, u], r3r.at[k, lat], dev).start()

    def lat_sum(k):
        for u in range(UNITS):
            @pl.when(jnp.logical_and(y < 3, unit_lat(k, u) == lat))
            def _():
                unit = st2[k, u].astype(F32)
                for d in range(1, nlat):
                    src = lax.rem(lat + d, nlat)
                    pltpu.make_async_copy(r3.at[k, src], r3.at[k, src], r3r.at[k, src]).wait()
                    unit = unit + r3[k, src].astype(F32)
                red[k, u] = unit.astype(BF)
                for d in range(1, nlat):
                    dev = {"segment": seg, "lat": lax.rem(lat + d, nlat), "dp": core}
                    remote(red.at[k, u], red.at[k, u], r4s.at[k, d], r4r.at[k, u], dev).start()

    my_piece = 3 * x_lo + jnp.minimum(y, 2)

    def deliver(k):
        @pl.when(y < 3)
        def _():
            for u in range(UNITS):
                @pl.when(unit_lat(k, u) != lat)
                def _():
                    pltpu.make_async_copy(red.at[k, u], red.at[k, u], r4r.at[k, u]).wait()

            @pl.when(seg == k)
            def _():
                gw_ref[core, my_piece] = red[k]

            @pl.when(seg != k)
            def _():
                dev = {"segment": k, "lat": lat, "dp": core}
                remote(red.at[k], gw_ref.at[core, my_piece], r5s.at[k], r5r.at[my_piece], dev).start()

    def staged(a):
        for lag, stage in ((2, pair_and_scatter), (4, sum_and_scatter), (6, lat_sum), (8, deliver)):
            k = a + lag

            @pl.when(jnp.logical_and(k >= 0, k < SECTIONS))
            def _():
                stage(k)

    def weight_work(k):
        later = k + SECTIONS
        taps = jnp.concatenate([tapped(gbuf[k + 1, 2]), tapped(gbuf[later + 1, 2])], axis=1)
        acts = jnp.concatenate([pbuf[k], pbuf[later]], axis=1)
        dw = lax.dot_general(taps, acts, (((1,), (1,)), ((), ())), preferred_element_type=F32)
        dwf[k] = dw.astype(BF).reshape(2, PIECES, piece, lanes)
        remote(dwf.at[k, other], cr.at[k], crs.at[k], crr.at[k], partner).start()
        staged(k)

    def adjoint_out(k):
        @pl.when(k < SECTIONS)
        def _():
            out_send(gbuf.at[k, 2], sa_ref, 1, k)

    def backward(t, with_weights):
        b = 2 * t + 1
        a = 2 * t
        step = APPS - 1 - t
        halo_start(gbuf, b + 1, step)
        if with_weights:
            adjoint_out(b + 2)
            adjoint_out(b + 1)
        else:
            @pl.when(b == APPS - 1)
            def _():
                state_out(jnp.int32(APPS - 1))
                state_out(jnp.int32(APPS))
        turned_weights(lax.rem(b, SECTIONS), 0)
        turned_weights(lax.rem(a, SECTIONS), 1)
        if with_weights:
            @pl.when(b < SECTIONS - 1)
            def _():
                weight_work(b + 1)

            weight_work(b)
        halo_wait(gbuf, b + 1, step)
        g = [gbuf[b + 1, i] for i in range(5)]
        sums = (
            jnp.dot(b2[0, 2], beside_each_other(g[1], g[2], g[3]), preferred_element_type=F32)
            + jnp.dot(b2[0, 0], beside_each_other(g[0], g[1], g[2]), preferred_element_type=F32)
            + jnp.dot(b2[0, 1], beside_each_other(g[2], g[3], g[4]), preferred_element_type=F32)
        )
        grads = []
        for m in range(3):
            moved = shifted_sum(sums[:, m * W : (m + 1) * W], 1)
            slope = silu_slope(sbuf[b, 1 + m].astype(F32))
            value = kept(m - 1, (g[1 + m].astype(F32) + slope * moved).astype(BF))
            gbuf[b, 1 + m] = value
            grads.append(value)
        sums = (
            jnp.dot(b2[1, 2], grads[1], preferred_element_type=F32)
            + jnp.dot(b2[1, 0], grads[0], preferred_element_type=F32)
            + jnp.dot(b2[1, 1], grads[2], preferred_element_type=F32)
        )
        slope = silu_slope(sbuf[a, 2].astype(F32))
        adjoint = grads[1].astype(F32) + slope * shifted_sum(sums, 1)
        if not with_weights:
            adjoint = adjoint + jnp.where(a == SECTIONS, xc[2].astype(F32), 0.0)
        gbuf[a, 2] = adjoint.astype(BF)

    def backward_late(i, carry):
        backward(APPS // 2 - 1 - i, False)
        return carry

    def backward_early(i, carry):
        backward(SECTIONS // 2 - 1 - i, True)
        return carry

    lax.fori_loop(0, (APPS - SECTIONS) // 2, backward_late, 0)
    lax.fori_loop(0, SECTIONS // 2, backward_early, 0)
    weight_work(jnp.int32(0))
    adjoint_out(jnp.int32(1))
    adjoint_out(jnp.int32(0))

    def drain(i, carry):
        staged(-1 - i)
        return carry

    lax.fori_loop(0, 8, drain, 0)
    for j in range(PIECES):
        @pl.when(seg != (j // 3) * 4 + j % 3)
        def _():
            pltpu.make_async_copy(gw_ref.at[core, j], gw_ref.at[core, j], r5r.at[j]).wait()
    last = remote(gw_ref.at[core], gw_ref.at[core], r6.at[0], r6.at[1], partner)
    last.start()

    for copy in sends:
        copy.wait_send()
    for j in range(4):
        beside_copy((1 - x_lo) * 4 + j).wait_send()
    for k in range(SECTIONS):
        for which, (dst, src) in enumerate(
            ((so_ref, sbuf.at[APPS - SECTIONS + k + 1, 2]), (sa_ref, gbuf.at[k, 2]))
        ):
            @pl.when(jnp.logical_not(is_self(k)))
            def _():
                out_copy(src, dst, which, k).wait_send()

    for what in range(2):
        for r in range(2):
            @pl.when(leaves(r))
            def _():
                given(r, what).wait_send()

    for s in range(8):
        from_self = jnp.logical_and(stays, jnp.logical_and(core == s % 2, y == s // 2))
        for which, dst in enumerate((so_ref, sa_ref)):
            @pl.when(jnp.logical_not(from_self))
            def _():
                pltpu.make_async_copy(dst.at[s], dst.at[s], ors.at[which, s]).wait()

    def ended(k, carry):
        pltpu.make_async_copy(dwf.at[k, other], dwf.at[k, other], crs.at[k]).wait()
        for j in range(PIECES):
            @pl.when(seg != (j // 3) * 4 + j % 3)
            def _():
                pltpu.make_async_copy(cs.at[k, j], cs.at[k, j], r2s.at[k, j]).wait()

        @pl.when(y < 3)
        def _():
            for u in range(UNITS):
                mine = unit_lat(k, u) == lat

                @pl.when(jnp.logical_not(mine))
                def _():
                    pltpu.make_async_copy(st2.at[k, u], st2.at[k, u], r3s.at[k, u]).wait()

                @pl.when(mine)
                def _():
                    for d in range(1, nlat):
                        pltpu.make_async_copy(red.at[k, u], red.at[k, u], r4s.at[k, d]).wait()

            @pl.when(seg != k)
            def _():
                pltpu.make_async_copy(red.at[k], red.at[k], r5s.at[k]).wait()

        return carry

    lax.fori_loop(0, SECTIONS, ended, 0)
    last.wait_send()
    pltpu.make_async_copy(gw_ref.at[other], gw_ref.at[other], r6.at[1]).wait()
    grads = gw_ref[...].reshape(K3, lanes).astype(F32) * normalizer
    for q in range(3):
        block = grads[q * C : (q + 1) * C]
        kg_ref[q] = block[:, 0:C]
        kg_ref[6 + q] = block[:, C : 2 * C]
        kg_ref[3 + q] = block[:, 2 * C : K3]
        if q == 1:
            bg_ref[...] = block[:, lanes - 128 :].T[K3 - lanes + 128 : K3 - lanes + 129]


def per_device(nz, initial, kernel, bias, cotangent):
    y = lax.rem(lax.axis_index("segment"), 4)
    C, W = initial.shape[1], initial.shape[3]
    K3 = 3 * C
    lanes = -(-(K3 + 2) // 128) * 128
    half, part = K3 // 2, K3 // 4
    nlat = 2 * nz
    piece = half // PIECES
    unit = piece // UNITS

    normalizer = 1.0 / math.sqrt(initial.shape[0] * 2 * initial.shape[2] * nlat * W)
    rows = jnp.stack([
        lax.dynamic_index_in_dim(band, y, 0, keepdims=False)
        for band in (initial, cotangent[1], cotangent[0])
    ]).transpose(2, 0, 1, 3)
    weights = kernel[0].transpose(1, 0, 2)
    offsets = jnp.broadcast_to(bias[0][:, None], (C, 128))

    vm = pl.BlockSpec(memory_space=pltpu.VMEM)
    dma = pltpu.SemaphoreType.DMA
    so, sa, kg, bg = pl.pallas_call(
        functools.partial(network_kernel, (C, W, nz), normalizer),
        out_shape=(
            jax.ShapeDtypeStruct((8, C, W), BF),
            jax.ShapeDtypeStruct((8, C, W), BF),
            jax.ShapeDtypeStruct((9, C, C), F32),
            jax.ShapeDtypeStruct((1, C), F32),
        ),
        in_specs=[vm, vm, vm],
        out_specs=(vm, vm, vm, vm),
        scratch_shapes=[
            pltpu.VMEM((2, PIECES, UNITS, unit, lanes), BF),
            pltpu.VMEM((3, C, W), BF),
            pltpu.VMEM((SECTIONS, 2, 2, part, lanes), BF),
            pltpu.VMEM((2, 3, K3, C), BF),
            pltpu.VMEM((APPS, lanes, W), BF),
            pltpu.VMEM((APPS + 1, 5, C, W), BF),
            pltpu.VMEM((APPS + 1, 5, C, W), BF),
            pltpu.VMEM((SECTIONS, 2, PIECES, piece, lanes), BF),
            pltpu.VMEM((SECTIONS, PIECES, piece, lanes), BF),
            pltpu.VMEM((SECTIONS, PIECES, piece, lanes), BF),
            pltpu.VMEM((SECTIONS, 8, piece, lanes), BF),
            pltpu.VMEM((SECTIONS, UNITS, unit, lanes), BF),
            pltpu.VMEM((SECTIONS, nlat, unit, lanes), BF),
            pltpu.VMEM((SECTIONS, UNITS, unit, lanes), BF),
            dma((2, 4)),
            dma((21,)),
            dma((22,)),
            dma((APPS, 5)),
            dma((APPS, 5)),
            dma((2, SECTIONS)),
            dma((2, 8)),
            dma((SECTIONS,)),
            dma((SECTIONS,)),
            dma((SECTIONS, PIECES)),
            dma((SECTIONS, 8)),
            dma((SECTIONS, UNITS)),
            dma((SECTIONS, nlat)),
            dma((SECTIONS, nlat)),
            dma((SECTIONS, UNITS)),
            dma((SECTIONS,)),
            dma((PIECES,)),
            dma((2,)),
        ],
        compiler_params=pltpu.CompilerParams(
            collective_id=0, has_side_effects=True, vmem_limit_bytes=60 * 2**20
        ),
    )(rows, weights, offsets)

    def banded(slots):
        return slots.reshape(4, 2, C, W).transpose(0, 2, 1, 3)[None]

    return (
        banded(so),
        banded(sa).astype(F32),
        kg.transpose(1, 0, 2)[None],
        bg,
    )


def solution(mesh):
    nz = mesh.shape["lat"] // 2
    return jax.shard_map(
        functools.partial(per_device, nz),
        mesh=mesh,
        in_specs=(
            P("dp", None, "lat", None),
            P("segment", None, None, None),
            P("segment", None),
            P(None, "dp", None, "lat", None),
        ),
        out_specs=(
            P("segment", "dp", None, "lat", None),
            P("segment", "dp", None, "lat", None),
            P("segment", None, None, None),
            P("segment", None),
        ),
        check_vma=False,
    )
```

```python
import functools
import math

import jax
import jax.numpy as jnp
from jax import lax
from jax.experimental import pallas as pl
from jax.experimental.pallas import tpu as pltpu
from jax.sharding import PartitionSpec as P

STEPS = 2
SECTIONS = 8
APPS = STEPS * SECTIONS
BF = jnp.bfloat16
F32 = jnp.float32
MESH = pl.DeviceIdType.MESH
REACH = (1, -1, 2, -2)


def silu_value(values):
    return values / (1.0 + jnp.exp(-values))


def silu_slope(values):
    sigmoid_v = 1.0 / (1.0 + jnp.exp(-values))
    return sigmoid_v * (1.0 + values * (1.0 - sigmoid_v))


PIECES = 6
UNITS = 3


def network_kernel(
    dims, normalizer, x_ref, w_ref, b_ref, so_ref, sa_ref, kg_ref, bg_ref,
    gw_ref, xc, wall, b2, pbuf, gbuf, sbuf, dwf, cr, cs, r2, st2, r3, red, xsem, wss, wrs,
    hss, hrs, oss, ors, crs, crr, r2s, r2r, r3s, r3r, r4s, r4r, r5s, r5r, r6,
):
    C, W, nz = dims
    K3 = 3 * C
    half = K3 // 2
    part = half // 2
    lanes = pbuf.shape[1]
    nlat = 2 * nz
    nrow = 4 * nz
    piece = half // PIECES

    seg = lax.axis_index("segment")
    lat = lax.axis_index("lat")
    core = lax.axis_index("dp")
    x_lo, y = seg // 4, lax.rem(seg, 4)
    z, x_hi = lat // 2, lax.rem(lat, 2)
    x = 2 * x_hi + x_lo
    odd = lax.rem(z, 2)
    held = lax.rem(x_lo + x_hi, 2)
    band = 2 * z + lax.rem(x_hi + odd, 2)
    row = 2 * band + core
    has_up = row > 0
    has_dn = row < nrow - 1

    def at(px, py, pz, pc=core):
        return {"segment": lax.rem(px, 2) * 4 + py, "lat": pz * 2 + px // 2, "dp": pc}

    def holder(r):
        r_band = r // 2
        rz = r_band // 2
        hi = lax.rem(r_band + rz, 2)
        return {"segment": lax.rem(held + hi, 2) * 4 + y, "lat": rz * 2 + hi, "dp": lax.rem(r, 2)}

    def inside(shift):
        return jnp.logical_and(row + shift >= 0, row + shift < nrow)

    other = 1 - core
    partner = {"segment": seg, "lat": lat, "dp": other}
    y_up, y_dn = lax.rem(y + 1, 4), lax.rem(y + 3, 4)
    x_up, x_dn = lax.rem(x + 1, 4), lax.rem(x + 3, 4)

    barrier = pltpu.get_barrier_semaphore()
    for d in range(1, 32):
        dx, dy, dc = d // 8, (d // 2) % 4, d % 2
        peer = at(lax.rem(x + dx, 4), lax.rem(y + dy, 4), z, lax.rem(core + dc, 2))
        pl.semaphore_signal(barrier, inc=1, device_id=peer, device_id_type=MESH)
    for d in range(1, nz):
        for hi in range(2):
            peer = {"segment": seg, "lat": lax.rem(z + d, nz) * 2 + hi, "dp": core}
            pl.semaphore_signal(barrier, inc=1, device_id=peer, device_id_type=MESH)
    for d in (1, nz - 1):
        peer = {"segment": seg, "lat": lax.rem(z + d, nz) * 2 + x_hi, "dp": other}
        pl.semaphore_signal(barrier, inc=1, device_id=peer, device_id_type=MESH)
    ones = (lax.broadcasted_iota(jnp.int32, (lanes - K3, W), 0) < 2).astype(F32).astype(BF)
    for shift in REACH:
        @pl.when(jnp.logical_not(inside(shift)))
        def _():
            @pl.loop(0, APPS // 2)
            def _(t):
                sbuf[2 * t, 2 + shift] = jnp.zeros((C, W), BF)
                gbuf[2 * t + 2, 2 + shift] = jnp.zeros((C, W), BF)

    lane = lax.broadcasted_iota(jnp.int32, (C, lanes - K3), 1)
    offsets = b_ref[:, 0 : lanes - K3]
    coarse = offsets.astype(BF).astype(F32)
    side = jnp.where(lane == 0, coarse, jnp.where(lane == 1, offsets - coarse, 0.0)).astype(BF)
    table = [
        jnp.concatenate(
            [w_ref[q], w_ref[6 + q], w_ref[3 + q], side if q == 1 else jnp.zeros_like(side)], axis=1
        )
        for q in range(3)
    ]
    wall[seg] = jnp.concatenate(table, axis=0).reshape(2, 2, part, lanes)
    pl.semaphore_wait(barrier, 31 + 2 * (nz - 1) + 2)

    def remote(src, dst, ssem, rsem, dev):
        return pltpu.make_async_remote_copy(
            src_ref=src, dst_ref=dst, send_sem=ssem, recv_sem=rsem, device_id=dev, device_id_type=MESH
        )

    giver = core == held
    stays = jnp.logical_and(giver, odd == 0)
    home_x = x + odd * (3 - 2 * x)

    def given(r, what):
        span = pl.ds(0, 1) if what == 0 else pl.ds(1, 2)
        return remote(
            x_ref.at[r, span], xc.at[span], xsem.at[0, 2 * r + what], xsem.at[1, what], at(home_x, y, z, r)
        )

    def leaves(r):
        return jnp.logical_and(giver, jnp.logical_or(odd == 1, core != r))

    for what in range(2):
        for r in range(2):
            @pl.when(leaves(r))
            def _():
                given(r, what).start()

    @pl.when(stays)
    def _():
        xc[...] = x_ref[core]

    def rows_wait(what):
        span = pl.ds(0, 1) if what == 0 else pl.ds(1, 2)

        @pl.when(jnp.logical_not(stays))
        def _():
            pltpu.make_async_copy(xc.at[span], xc.at[span], xsem.at[1, what]).wait()

    sec_dn, sec_up = x_lo * 4 + y_dn, x_lo * 4 + y_up
    sec_far = x_lo * 4 + lax.rem(y + 2, 4)
    sends = []

    def go(copy):
        copy.start()
        sends.append(copy)

    def send_w(index, src, slot, dev):
        go(remote(src, src, wss.at[index], wrs.at[slot], dev))

    dev_yu, dev_yd = at(x, y_up, z), at(x, y_dn, z)
    dev_xu, dev_xd = at(x_up, y, z), at(x_dn, y, z)
    send_w(0, wall.at[seg, core, 0], 0, dev_yu)
    send_w(1, wall.at[seg, core, 1], 1, dev_yd)
    send_w(2, wall.at[seg, core, 0], 4 + 2 * y, dev_xu)
    send_w(3, wall.at[seg, core, 1], 5 + 2 * y, dev_xd)
    send_w(19, wall.at[seg, core, 1], 20, dev_yu)
    send_w(20, wall.at[seg, core, 0], 21, dev_yd)

    def landed(ref, slot):
        pltpu.make_async_copy(ref, ref, wrs.at[slot]).wait()

    def halo_copy(buf, slot, step, shift):
        return remote(
            buf.at[slot, 2], buf.at[slot, 2 - shift], hss.at[step, 2 + shift], hrs.at[step, 2 - shift],
            holder(jnp.clip(row + shift, 0, nrow - 1)),
        )

    def halo_start(buf, slot, step):
        for shift in REACH:
            @pl.when(inside(shift))
            def _():
                halo_copy(buf, slot, step, shift).start()

    def halo_wait(buf, slot, step):
        for shift in REACH:
            @pl.when(inside(shift))
            def _():
                there = buf.at[slot, 2 + shift]
                pltpu.make_async_copy(there, there, hrs.at[step, 2 + shift]).wait()

        for shift in REACH:
            @pl.when(inside(shift))
            def _():
                halo_copy(buf, slot, step, shift).wait_send()

    rows_wait(0)
    sbuf[0, 2] = xc[0]
    halo_start(sbuf, 0, 0)

    def across(index, sec, part_at):
        slot = 4 + 2 * lax.rem(sec, 4) + part_at
        send_w(index, wall.at[sec, core, part_at], slot, dev_xu if part_at == 0 else dev_xd)

    def beside(index, sec):
        send_w(index, wall.at[sec, core], 12 + sec, partner)

    landed(wall.at[sec_dn, core, 0], 0)
    send_w(4, wall.at[sec_dn, core, 0], 2, dev_yu)
    across(5, sec_dn, 0)
    landed(wall.at[sec_up, core, 1], 1)
    send_w(8, wall.at[sec_up, core, 1], 3, dev_yd)
    across(10, sec_up, 1)
    landed(wall.at[sec_dn, core, 1], 20)
    across(6, sec_dn, 1)
    beside(7, sec_dn)
    landed(wall.at[sec_up, core, 0], 21)
    across(9, sec_up, 0)
    beside(11, sec_up)
    landed(wall.at[sec_far, core, 0], 2)
    across(12, sec_far, 0)
    landed(wall.at[sec_far, core, 1], 3)
    across(13, sec_far, 1)
    beside(14, sec_far)

    def beside_copy(sec):
        half_ref = wall.at[sec, core]
        return remote(half_ref, half_ref, wss.at[15 + lax.rem(sec, 4)], wrs.at[12 + sec], partner)

    def take_section(sec):
        @pl.when(jnp.logical_and(sec < SECTIONS, sec // 4 != x_lo))
        def _():
            sy = lax.rem(sec, 4)
            landed(wall.at[sec, core, 0], 4 + 2 * sy)
            landed(wall.at[sec, core, 1], 5 + 2 * sy)
            beside_copy(sec).start()

    def need_section(sec):
        @pl.when(jnp.logical_and(sec < SECTIONS, sec != seg))
        def _():
            landed(wall.at[sec, other], 12 + sec)

    take_section(jnp.int32(0))
    take_section(jnp.int32(1))
    out_slot = y * 2 + core

    def out_copy(src, dst, which, k):
        dev = {"segment": k, "lat": band, "dp": held}
        return remote(src, dst.at[out_slot], oss.at[which, k], ors.at[which, out_slot], dev)

    def is_self(k):
        return jnp.logical_and(seg == k, stays)

    def out_send(src, dst, which, k):
        mine = is_self(k)

        @pl.when(mine)
        def _():
            dst[out_slot] = src[...]

        @pl.when(jnp.logical_not(mine))
        def _():
            out_copy(src, dst, which, k).start()

    def shifted_sum(parts, sign):
        minus, same, plus = parts[0:C], parts[C : 2 * C], parts[2 * C :]
        return same + pltpu.roll(minus, 1 if sign < 0 else W - 1, 1) + pltpu.roll(plus, W - 1 if sign < 0 else 1, 1)

    def kept(shift, values):
        return jnp.where(inside(shift), values, jnp.zeros_like(values))

    def beside_each_other(*blocks):
        return jnp.concatenate(blocks, axis=1)

    def activated(state):
        return silu_value(state.astype(F32)).astype(BF)

    def state_out(number):
        @pl.when(number > APPS - SECTIONS)
        def _():
            out_send(sbuf.at[number, 2], so_ref, 0, number - 1 - (APPS - SECTIONS))

    def forward(t, carry):
        a = 2 * t

        @pl.when(t > 0)
        def _():
            halo_start(sbuf, a, t)

        take_section(a + 2)
        take_section(a + 3)
        state_out(a - 1)
        state_out(a)
        need_section(a)
        need_section(a + 1)
        k = lax.rem(a, SECTIONS)
        table = wall[k].reshape(K3, lanes)
        halo_wait(sbuf, a, t)
        acts = [activated(sbuf[a, i]) for i in range(5)]
        pbuf[a] = jnp.concatenate([acts[1], acts[3], acts[2], ones], axis=0)
        wide = jnp.concatenate(
            [
                beside_each_other(acts[0], acts[1], acts[2]),
                beside_each_other(acts[2], acts[3], acts[4]),
                beside_each_other(acts[1], acts[2], acts[3]),
                beside_each_other(ones, ones, ones),
            ],
            axis=0,
        )
        sums = jnp.dot(table, wide, preferred_element_type=F32)
        nexts = []
        for m in range(3):
            branch = shifted_sum(sums[:, m * W : (m + 1) * W], -1)
            value = kept(m - 1, (sbuf[a, 1 + m].astype(F32) + branch).astype(BF))
            sbuf[a + 1, 1 + m] = value
            nexts.append(value)
        acts = [activated(value) for value in nexts]
        column = jnp.concatenate([acts[0], acts[2], acts[1], ones], axis=0)
        pbuf[a + 1] = column
        sums = jnp.dot(wall[lax.rem(a + 1, SECTIONS)].reshape(K3, lanes), column, preferred_element_type=F32)
        sbuf[a + 2, 2] = (nexts[1].astype(F32) + shifted_sum(sums, -1)).astype(BF)
        return carry

    lax.fori_loop(0, APPS // 2, forward, 0)

    rows_wait(1)
    gbuf[APPS, 2] = xc[1]

    def turned_weights(k, which):
        table = wall[k].reshape(K3, lanes)
        for q in range(3):
            turned = table[q * C : (q + 1) * C, :K3].T
            b2[which, 1, q * C : (q + 1) * C, :] = turned[0:C]
            b2[which, 0, q * C : (q + 1) * C, :] = turned[C : 2 * C]
            b2[which, 2, q * C : (q + 1) * C, :] = turned[2 * C :]

    def tapped(grad):
        wide = grad.astype(F32)
        return jnp.concatenate(
            [pltpu.roll(wide, W - 1, 1).astype(BF), grad, pltpu.roll(wide, 1, 1).astype(BF)], axis=0
        )

    def pair_and_scatter(k):
        pltpu.make_async_copy(cr.at[k], cr.at[k], crr.at[k]).wait()
        for jx in range(2):
            for jy in range(3):
                j = 3 * jx + jy
                cs[k, j] = (dwf[k, core, j].astype(F32) + cr[k, j].astype(F32)).astype(BF)
                near = x_lo == jx
                far_x = x + 1 - 2 * x_lo
                home = at(jnp.where(near, x, far_x), jy, z)
                slot = jnp.where(near, y, 4 + y)
                mine = jnp.logical_and(near, y == jy)

                @pl.when(mine)
                def _():
                    r2[k, slot] = cs[k, j]

                @pl.when(jnp.logical_not(mine))
                def _():
                    remote(cs.at[k, j], r2.at[k, slot], r2s.at[k, j], r2r.at[k, slot], home).start()

    def unit_lat(k, u):
        return lax.rem((nlat // 3) * u + 2 * k, nlat)

    def sum_and_scatter(k):
        @pl.when(y < 3)
        def _():
            total = r2[k, y].astype(F32)
            for d in range(1, 4):
                src = lax.rem(y + d, 4)
                pltpu.make_async_copy(r2.at[k, src], r2.at[k, src], r2r.at[k, src]).wait()
                total = total + r2[k, src].astype(F32)
            for src in range(4, 8):
                pltpu.make_async_copy(r2.at[k, src], r2.at[k, src], r2r.at[k, src]).wait()
                total = total + r2[k, src].astype(F32)
            st2[k] = total.astype(BF).reshape(UNITS, piece // UNITS, lanes)
            for u in range(UNITS):
                goal = unit_lat(k, u)

                @pl.when(goal != lat)
                def _():
                    dev = {"segment": seg, "lat": goal, "dp": core}
                    remote(st2.at[k, u], r3.at[k, lat], r3s.at[k, u], r3r.at[k, lat], dev).start()

    def lat_sum(k):
        for u in range(UNITS):
            @pl.when(jnp.logical_and(y < 3, unit_lat(k, u) == lat))
            def _():
                unit = st2[k, u].astype(F32)
                for d in range(1, nlat):
                    src = lax.rem(lat + d, nlat)
                    pltpu.make_async_copy(r3.at[k, src], r3.at[k, src], r3r.at[k, src]).wait()
                    unit = unit + r3[k, src].astype(F32)
                red[k, u] = unit.astype(BF)
                for d in range(1, nlat):
                    dev = {"segment": seg, "lat": lax.rem(lat + d, nlat), "dp": core}
                    remote(red.at[k, u], red.at[k, u], r4s.at[k, d], r4r.at[k, u], dev).start()

    my_piece = 3 * x_lo + jnp.minimum(y, 2)

    def deliver(k):
        @pl.when(y < 3)
        def _():
            for u in range(UNITS):
                @pl.when(unit_lat(k, u) != lat)
                def _():
                    pltpu.make_async_copy(red.at[k, u], red.at[k, u], r4r.at[k, u]).wait()

            @pl.when(seg == k)
            def _():
                gw_ref[core, my_piece] = red[k]

            @pl.when(seg != k)
            def _():
                dev = {"segment": k, "lat": lat, "dp": core}
                remote(red.at[k], gw_ref.at[core, my_piece], r5s.at[k], r5r.at[my_piece], dev).start()

    def staged(a, first=0):
        for lag, stage in ((1, pair_and_scatter), (4, sum_and_scatter), (6, lat_sum), (8, deliver))[first:]:
            k = a + lag

            @pl.when(jnp.logical_and(k >= 0, k < SECTIONS))
            def _():
                stage(k)

    def weight_work(k):
        later = k + SECTIONS
        taps = jnp.concatenate([tapped(gbuf[k + 1, 2]), tapped(gbuf[later + 1, 2])], axis=1)
        acts = jnp.concatenate([pbuf[k], pbuf[later]], axis=1)
        dw = lax.dot_general(taps, acts, (((1,), (1,)), ((), ())), preferred_element_type=F32)
        dwf[k] = dw.astype(BF).reshape(2, PIECES, piece, lanes)
        remote(dwf.at[k, other], cr.at[k], crs.at[k], crr.at[k], partner).start()

    def adjoint_out(k):
        @pl.when(k < SECTIONS)
        def _():
            out_send(gbuf.at[k, 2], sa_ref, 1, k)

    def backward(t, with_weights):
        b = 2 * t + 1
        a = 2 * t
        step = APPS - 1 - t
        halo_start(gbuf, b + 1, step)
        if with_weights:
            adjoint_out(b + 2)
            adjoint_out(b + 1)
        else:
            @pl.when(b == APPS - 1)
            def _():
                state_out(jnp.int32(APPS - 1))
                state_out(jnp.int32(APPS))
        turned_weights(lax.rem(b, SECTIONS), 0)
        turned_weights(lax.rem(a, SECTIONS), 1)
        if with_weights:
            @pl.when(b < SECTIONS - 1)
            def _():
                weight_work(b + 1)
                staged(b + 1)

            weight_work(b)
            staged(b)
        halo_wait(gbuf, b + 1, step)
        g = [gbuf[b + 1, i] for i in range(5)]
        sums = (
            jnp.dot(b2[0, 2], beside_each_other(g[1], g[2], g[3]), preferred_element_type=F32)
            + jnp.dot(b2[0, 0], beside_each_other(g[0], g[1], g[2]), preferred_element_type=F32)
            + jnp.dot(b2[0, 1], beside_each_other(g[2], g[3], g[4]), preferred_element_type=F32)
        )
        grads = []
        for m in range(3):
            moved = shifted_sum(sums[:, m * W : (m + 1) * W], 1)
            slope = silu_slope(sbuf[b, 1 + m].astype(F32))
            value = kept(m - 1, (g[1 + m].astype(F32) + slope * moved).astype(BF))
            gbuf[b, 1 + m] = value
            grads.append(value)
        sums = (
            jnp.dot(b2[1, 2], grads[1], preferred_element_type=F32)
            + jnp.dot(b2[1, 0], grads[0], preferred_element_type=F32)
            + jnp.dot(b2[1, 1], grads[2], preferred_element_type=F32)
        )
        slope = silu_slope(sbuf[a, 2].astype(F32))
        adjoint = grads[1].astype(F32) + slope * shifted_sum(sums, 1)
        if not with_weights:
            adjoint = adjoint + jnp.where(a == SECTIONS, xc[2].astype(F32), 0.0)
        gbuf[a, 2] = adjoint.astype(BF)

    def backward_late(i, carry):
        backward(APPS // 2 - 1 - i, False)
        return carry

    def backward_early(i, carry):
        backward(SECTIONS // 2 - 1 - i, True)
        return carry

    lax.fori_loop(0, (APPS - SECTIONS) // 2, backward_late, 0)
    lax.fori_loop(0, SECTIONS // 2, backward_early, 0)
    weight_work(jnp.int32(0))
    pair_and_scatter(jnp.int32(1))
    pair_and_scatter(jnp.int32(0))
    adjoint_out(jnp.int32(1))
    adjoint_out(jnp.int32(0))
    staged(jnp.int32(0), 1)

    def drain(i, carry):
        staged(-1 - i, 1)
        return carry

    lax.fori_loop(0, 8, drain, 0)
    for j in range(PIECES):
        @pl.when(seg != (j // 3) * 4 + j % 3)
        def _():
            pltpu.make_async_copy(gw_ref.at[core, j], gw_ref.at[core, j], r5r.at[j]).wait()
    last = remote(gw_ref.at[core], gw_ref.at[core], r6.at[0], r6.at[1], partner)
    last.start()

    for copy in sends:
        copy.wait_send()
    for j in range(4):
        beside_copy((1 - x_lo) * 4 + j).wait_send()
    for k in range(SECTIONS):
        for which, (dst, src) in enumerate(
            ((so_ref, sbuf.at[APPS - SECTIONS + k + 1, 2]), (sa_ref, gbuf.at[k, 2]))
        ):
            @pl.when(jnp.logical_not(is_self(k)))
            def _():
                out_copy(src, dst, which, k).wait_send()

    for what in range(2):
        for r in range(2):
            @pl.when(leaves(r))
            def _():
                given(r, what).wait_send()

    for s in range(8):
        from_self = jnp.logical_and(stays, jnp.logical_and(core == s % 2, y == s // 2))
        for which, dst in enumerate((so_ref, sa_ref)):
            @pl.when(jnp.logical_not(from_self))
            def _():
                pltpu.make_async_copy(dst.at[s], dst.at[s], ors.at[which, s]).wait()

    def ended(k, carry):
        pltpu.make_async_copy(dwf.at[k, other], dwf.at[k, other], crs.at[k]).wait()
        for j in range(PIECES):
            @pl.when(seg != (j // 3) * 4 + j % 3)
            def _():
                pltpu.make_async_copy(cs.at[k, j], cs.at[k, j], r2s.at[k, j]).wait()

        @pl.when(y < 3)
        def _():
            for u in range(UNITS):
                mine = unit_lat(k, u) == lat

                @pl.when(jnp.logical_not(mine))
                def _():
                    pltpu.make_async_copy(st2.at[k, u], st2.at[k, u], r3s.at[k, u]).wait()

                @pl.when(mine)
                def _():
                    for d in range(1, nlat):
                        pltpu.make_async_copy(red.at[k, u], red.at[k, u], r4s.at[k, d]).wait()

            @pl.when(seg != k)
            def _():
                pltpu.make_async_copy(red.at[k], red.at[k], r5s.at[k]).wait()

        return carry

    lax.fori_loop(0, SECTIONS, ended, 0)
    last.wait_send()
    pltpu.make_async_copy(gw_ref.at[other], gw_ref.at[other], r6.at[1]).wait()
    grads = gw_ref[...].reshape(K3, lanes).astype(F32) * normalizer
    for q in range(3):
        block = grads[q * C : (q + 1) * C]
        kg_ref[q] = block[:, 0:C]
        kg_ref[6 + q] = block[:, C : 2 * C]
        kg_ref[3 + q] = block[:, 2 * C : K3]
        if q == 1:
            bg_ref[...] = block[:, lanes - 128 :].T[K3 - lanes + 128 : K3 - lanes + 129]


def per_device(nz, initial, kernel, bias, cotangent):
    y = lax.rem(lax.axis_index("segment"), 4)
    C, W = initial.shape[1], initial.shape[3]
    K3 = 3 * C
    lanes = -(-(K3 + 2) // 128) * 128
    half, part = K3 // 2, K3 // 4
    nlat = 2 * nz
    piece = half // PIECES
    unit = piece // UNITS

    normalizer = 1.0 / math.sqrt(initial.shape[0] * 2 * initial.shape[2] * nlat * W)
    rows = jnp.stack([
        lax.dynamic_index_in_dim(band, y, 0, keepdims=False)
        for band in (initial, cotangent[1], cotangent[0])
    ]).transpose(2, 0, 1, 3)
    weights = kernel[0].transpose(1, 0, 2)
    offsets = jnp.broadcast_to(bias[0][:, None], (C, 128))

    vm = pl.BlockSpec(memory_space=pltpu.VMEM)
    dma = pltpu.SemaphoreType.DMA
    so, sa, kg, bg = pl.pallas_call(
        functools.partial(network_kernel, (C, W, nz), normalizer),
        out_shape=(
            jax.ShapeDtypeStruct((8, C, W), BF),
            jax.ShapeDtypeStruct((8, C, W), BF),
            jax.ShapeDtypeStruct((9, C, C), F32),
            jax.ShapeDtypeStruct((1, C), F32),
        ),
        in_specs=[vm, vm, vm],
        out_specs=(vm, vm, vm, vm),
        scratch_shapes=[
            pltpu.VMEM((2, PIECES, UNITS, unit, lanes), BF),
            pltpu.VMEM((3, C, W), BF),
            pltpu.VMEM((SECTIONS, 2, 2, part, lanes), BF),
            pltpu.VMEM((2, 3, K3, C), BF),
            pltpu.VMEM((APPS, lanes, W), BF),
            pltpu.VMEM((APPS + 1, 5, C, W), BF),
            pltpu.VMEM((APPS + 1, 5, C, W), BF),
            pltpu.VMEM((SECTIONS, 2, PIECES, piece, lanes), BF),
            pltpu.VMEM((SECTIONS, PIECES, piece, lanes), BF),
            pltpu.VMEM((SECTIONS, PIECES, piece, lanes), BF),
            pltpu.VMEM((SECTIONS, 8, piece, lanes), BF),
            pltpu.VMEM((SECTIONS, UNITS, unit, lanes), BF),
            pltpu.VMEM((SECTIONS, nlat, unit, lanes), BF),
            pltpu.VMEM((SECTIONS, UNITS, unit, lanes), BF),
            dma((2, 4)),
            dma((21,)),
            dma((22,)),
            dma((APPS, 5)),
            dma((APPS, 5)),
            dma((2, SECTIONS)),
            dma((2, 8)),
            dma((SECTIONS,)),
            dma((SECTIONS,)),
            dma((SECTIONS, PIECES)),
            dma((SECTIONS, 8)),
            dma((SECTIONS, UNITS)),
            dma((SECTIONS, nlat)),
            dma((SECTIONS, nlat)),
            dma((SECTIONS, UNITS)),
            dma((SECTIONS,)),
            dma((PIECES,)),
            dma((2,)),
        ],
        compiler_params=pltpu.CompilerParams(
            collective_id=0, has_side_effects=True, vmem_limit_bytes=60 * 2**20
        ),
    )(rows, weights, offsets)

    def banded(slots):
        return slots.reshape(4, 2, C, W).transpose(0, 2, 1, 3)[None]

    return (
        banded(so),
        banded(sa).astype(F32),
        kg.transpose(1, 0, 2)[None],
        bg,
    )


def solution(mesh):
    nz = mesh.shape["lat"] // 2
    return jax.shard_map(
        functools.partial(per_device, nz),
        mesh=mesh,
        in_specs=(
            P("dp", None, "lat", None),
            P("segment", None, None, None),
            P("segment", None),
            P(None, "dp", None, "lat", None),
        ),
        out_specs=(
            P("segment", "dp", None, "lat", None),
            P("segment", "dp", None, "lat", None),
            P("segment", None, None, None),
            P("segment", None),
        ),
        check_vma=False,
    )
```

```python
import functools
import math

import jax
import jax.numpy as jnp
from jax import lax
from jax.experimental import pallas as pl
from jax.experimental.pallas import tpu as pltpu
from jax.sharding import PartitionSpec as P

STEPS = 2
SECTIONS = 8
APPS = STEPS * SECTIONS
BF = jnp.bfloat16
F32 = jnp.float32
MESH = pl.DeviceIdType.MESH
REACH = (1, -1, 2, -2)


def silu_value(values):
    return values / (1.0 + jnp.exp(-values))


def silu_slope(values):
    sigmoid_v = 1.0 / (1.0 + jnp.exp(-values))
    return sigmoid_v * (1.0 + values * (1.0 - sigmoid_v))


PIECES = 6
UNITS = 3


def network_kernel(
    dims, normalizer, x_ref, w_ref, b_ref, so_ref, sa_ref, kg_ref, bg_ref,
    gw_ref, xc, wall, b2, pbuf, gbuf, sbuf, dwf, cr, cs, r2, st2, r3, red, xsem, wss, wrs,
    hss, hrs, oss, ors, crs, crr, r2s, r2r, r3s, r3r, r4s, r4r, r5s, r5r, r6,
):
    C, W, nz = dims
    K3 = 3 * C
    half = K3 // 2
    part = half // 2
    lanes = pbuf.shape[1]
    nlat = 2 * nz
    nrow = 4 * nz
    piece = half // PIECES

    seg = lax.axis_index("segment")
    lat = lax.axis_index("lat")
    core = lax.axis_index("dp")
    x_lo, y = seg // 4, lax.rem(seg, 4)
    z, x_hi = lat // 2, lax.rem(lat, 2)
    x = 2 * x_hi + x_lo
    odd = lax.rem(z, 2)
    held = lax.rem(x_lo + x_hi, 2)
    band = 2 * z + lax.rem(x_hi + odd, 2)
    row = 2 * band + core
    has_up = row > 0
    has_dn = row < nrow - 1

    def at(px, py, pz, pc=core):
        return {"segment": lax.rem(px, 2) * 4 + py, "lat": pz * 2 + px // 2, "dp": pc}

    def holder(r):
        r_band = r // 2
        rz = r_band // 2
        hi = lax.rem(r_band + rz, 2)
        return {"segment": lax.rem(held + hi, 2) * 4 + y, "lat": rz * 2 + hi, "dp": lax.rem(r, 2)}

    def inside(shift):
        return jnp.logical_and(row + shift >= 0, row + shift < nrow)

    other = 1 - core
    partner = {"segment": seg, "lat": lat, "dp": other}
    y_up, y_dn = lax.rem(y + 1, 4), lax.rem(y + 3, 4)
    x_up, x_dn = lax.rem(x + 1, 4), lax.rem(x + 3, 4)

    barrier = pltpu.get_barrier_semaphore()
    for d in range(1, 32):
        dx, dy, dc = d // 8, (d // 2) % 4, d % 2
        peer = at(lax.rem(x + dx, 4), lax.rem(y + dy, 4), z, lax.rem(core + dc, 2))
        pl.semaphore_signal(barrier, inc=1, device_id=peer, device_id_type=MESH)
    for d in range(1, nz):
        for hi in range(2):
            peer = {"segment": seg, "lat": lax.rem(z + d, nz) * 2 + hi, "dp": core}
            pl.semaphore_signal(barrier, inc=1, device_id=peer, device_id_type=MESH)
    for d in (1, nz - 1):
        peer = {"segment": seg, "lat": lax.rem(z + d, nz) * 2 + x_hi, "dp": other}
        pl.semaphore_signal(barrier, inc=1, device_id=peer, device_id_type=MESH)
    ones = (lax.broadcasted_iota(jnp.int32, (lanes - K3, W), 0) < 2).astype(F32).astype(BF)
    for shift in REACH:
        @pl.when(jnp.logical_not(inside(shift)))
        def _():
            @pl.loop(0, APPS // 2)
            def _(t):
                sbuf[2 * t, 2 + shift] = jnp.zeros((C, W), BF)
                gbuf[2 * t + 2, 2 + shift] = jnp.zeros((C, W), BF)

    lane = lax.broadcasted_iota(jnp.int32, (C, lanes - K3), 1)
    offsets = b_ref[:, 0 : lanes - K3]
    coarse = offsets.astype(BF).astype(F32)
    side = jnp.where(lane == 0, coarse, jnp.where(lane == 1, offsets - coarse, 0.0)).astype(BF)
    table = [
        jnp.concatenate(
            [w_ref[q], w_ref[6 + q], w_ref[3 + q], side if q == 1 else jnp.zeros_like(side)], axis=1
        )
        for q in range(3)
    ]
    wall[seg] = jnp.concatenate(table, axis=0).reshape(2, 2, part, lanes)
    pl.semaphore_wait(barrier, 31 + 2 * (nz - 1) + 2)

    def remote(src, dst, ssem, rsem, dev):
        return pltpu.make_async_remote_copy(
            src_ref=src, dst_ref=dst, send_sem=ssem, recv_sem=rsem, device_id=dev, device_id_type=MESH
        )

    giver = core == held
    stays = jnp.logical_and(giver, odd == 0)
    home_x = x + odd * (3 - 2 * x)

    def given(r, what):
        span = pl.ds(0, 1) if what == 0 else pl.ds(1, 2)
        return remote(
            x_ref.at[r, span], xc.at[span], xsem.at[0, 2 * r + what], xsem.at[1, what], at(home_x, y, z, r)
        )

    def leaves(r):
        return jnp.logical_and(giver, jnp.logical_or(odd == 1, core != r))

    for what in range(2):
        for r in range(2):
            @pl.when(leaves(r))
            def _():
                given(r, what).start()

    @pl.when(stays)
    def _():
        xc[...] = x_ref[core]

    def rows_wait(what):
        span = pl.ds(0, 1) if what == 0 else pl.ds(1, 2)

        @pl.when(jnp.logical_not(stays))
        def _():
            pltpu.make_async_copy(xc.at[span], xc.at[span], xsem.at[1, what]).wait()

    sec_dn, sec_up = x_lo * 4 + y_dn, x_lo * 4 + y_up
    sec_far = x_lo * 4 + lax.rem(y + 2, 4)
    sends = []

    def go(copy):
        copy.start()
        sends.append(copy)

    def send_w(index, src, slot, dev):
        go(remote(src, src, wss.at[index], wrs.at[slot], dev))

    dev_yu, dev_yd = at(x, y_up, z), at(x, y_dn, z)
    dev_xu, dev_xd = at(x_up, y, z), at(x_dn, y, z)
    send_w(0, wall.at[seg, core, 0], 0, dev_yu)
    send_w(1, wall.at[seg, core, 1], 1, dev_yd)
    send_w(2, wall.at[seg, core, 0], 4 + 2 * y, dev_xu)
    send_w(3, wall.at[seg, core, 1], 5 + 2 * y, dev_xd)
    send_w(19, wall.at[seg, core, 1], 20, dev_yu)
    send_w(20, wall.at[seg, core, 0], 21, dev_yd)

    def landed(ref, slot):
        pltpu.make_async_copy(ref, ref, wrs.at[slot]).wait()

    def halo_copy(buf, slot, step, shift):
        return remote(
            buf.at[slot, 2], buf.at[slot, 2 - shift], hss.at[step, 2 + shift], hrs.at[step, 2 - shift],
            holder(jnp.clip(row + shift, 0, nrow - 1)),
        )

    def halo_start(buf, slot, step):
        for shift in REACH:
            @pl.when(inside(shift))
            def _():
                halo_copy(buf, slot, step, shift).start()

    def halo_wait(buf, slot, step):
        for shift in REACH:
            @pl.when(inside(shift))
            def _():
                there = buf.at[slot, 2 + shift]
                pltpu.make_async_copy(there, there, hrs.at[step, 2 + shift]).wait()

        for shift in REACH:
            @pl.when(inside(shift))
            def _():
                halo_copy(buf, slot, step, shift).wait_send()

    rows_wait(0)
    sbuf[0, 2] = xc[0]
    halo_start(sbuf, 0, 0)

    def across(index, sec, part_at):
        slot = 4 + 2 * lax.rem(sec, 4) + part_at
        send_w(index, wall.at[sec, core, part_at], slot, dev_xu if part_at == 0 else dev_xd)

    def beside(index, sec):
        send_w(index, wall.at[sec, core], 12 + sec, partner)

    landed(wall.at[sec_dn, core, 0], 0)
    send_w(4, wall.at[sec_dn, core, 0], 2, dev_yu)
    across(5, sec_dn, 0)
    landed(wall.at[sec_up, core, 1], 1)
    send_w(8, wall.at[sec_up, core, 1], 3, dev_yd)
    across(10, sec_up, 1)
    landed(wall.at[sec_dn, core, 1], 20)
    across(6, sec_dn, 1)
    beside(7, sec_dn)
    landed(wall.at[sec_up, core, 0], 21)
    across(9, sec_up, 0)
    beside(11, sec_up)
    landed(wall.at[sec_far, core, 0], 2)
    across(12, sec_far, 0)
    landed(wall.at[sec_far, core, 1], 3)
    across(13, sec_far, 1)
    beside(14, sec_far)

    def beside_copy(sec):
        half_ref = wall.at[sec, core]
        return remote(half_ref, half_ref, wss.at[15 + lax.rem(sec, 4)], wrs.at[12 + sec], partner)

    def take_section(sec):
        @pl.when(jnp.logical_and(sec < SECTIONS, sec // 4 != x_lo))
        def _():
            sy = lax.rem(sec, 4)
            landed(wall.at[sec, core, 0], 4 + 2 * sy)
            landed(wall.at[sec, core, 1], 5 + 2 * sy)
            beside_copy(sec).start()

    def need_section(sec):
        @pl.when(jnp.logical_and(sec < SECTIONS, sec != seg))
        def _():
            landed(wall.at[sec, other], 12 + sec)

    take_section(jnp.int32(0))
    take_section(jnp.int32(1))
    out_slot = y * 2 + core

    def out_copy(src, dst, which, k):
        dev = {"segment": k, "lat": band, "dp": held}
        return remote(src, dst.at[out_slot], oss.at[which, k], ors.at[which, out_slot], dev)

    def is_self(k):
        return jnp.logical_and(seg == k, stays)

    def out_send(src, dst, which, k):
        mine = is_self(k)

        @pl.when(mine)
        def _():
            dst[out_slot] = src[...]

        @pl.when(jnp.logical_not(mine))
        def _():
            out_copy(src, dst, which, k).start()

    def shifted_sum(parts, sign):
        minus, same, plus = parts[0:C], parts[C : 2 * C], parts[2 * C :]
        return same + pltpu.roll(minus, 1 if sign < 0 else W - 1, 1) + pltpu.roll(plus, W - 1 if sign < 0 else 1, 1)

    def kept(shift, values):
        return jnp.where(inside(shift), values, jnp.zeros_like(values))

    def beside_each_other(*blocks):
        return jnp.concatenate(blocks, axis=1)

    def activated(state):
        return silu_value(state.astype(F32)).astype(BF)

    def state_out(number):
        @pl.when(number > APPS - SECTIONS)
        def _():
            out_send(sbuf.at[number, 2], so_ref, 0, number - 1 - (APPS - SECTIONS))

    def forward(t, carry):
        a = 2 * t

        @pl.when(t > 0)
        def _():
            halo_start(sbuf, a, t)

        take_section(a + 2)
        take_section(a + 3)
        state_out(a - 1)
        state_out(a)
        need_section(a)
        need_section(a + 1)
        k = lax.rem(a, SECTIONS)
        table = wall[k].reshape(K3, lanes)
        halo_wait(sbuf, a, t)
        acts = [activated(sbuf[a, i]) for i in range(5)]
        pbuf[a] = jnp.concatenate([acts[1], acts[3], acts[2], ones], axis=0)
        wide = jnp.concatenate(
            [
                beside_each_other(acts[0], acts[1], acts[2]),
                beside_each_other(acts[2], acts[3], acts[4]),
                beside_each_other(acts[1], acts[2], acts[3]),
                beside_each_other(ones, ones, ones),
            ],
            axis=0,
        )
        sums = jnp.dot(table, wide, preferred_element_type=F32)
        nexts = []
        for m in range(3):
            branch = shifted_sum(sums[:, m * W : (m + 1) * W], -1)
            value = kept(m - 1, (sbuf[a, 1 + m].astype(F32) + branch).astype(BF))
            sbuf[a + 1, 1 + m] = value
            nexts.append(value)
        acts = [activated(value) for value in nexts]
        column = jnp.concatenate([acts[0], acts[2], acts[1], ones], axis=0)
        pbuf[a + 1] = column
        sums = jnp.dot(wall[lax.rem(a + 1, SECTIONS)].reshape(K3, lanes), column, preferred_element_type=F32)
        sbuf[a + 2, 2] = (nexts[1].astype(F32) + shifted_sum(sums, -1)).astype(BF)
        return carry

    lax.fori_loop(0, APPS // 2, forward, 0)

    rows_wait(1)
    gbuf[APPS, 2] = xc[1]

    def turned_weights(k, which):
        table = wall[k].reshape(K3, lanes)
        for q in range(3):
            turned = table[q * C : (q + 1) * C, :K3].T
            b2[which, 1, q * C : (q + 1) * C, :] = turned[0:C]
            b2[which, 0, q * C : (q + 1) * C, :] = turned[C : 2 * C]
            b2[which, 2, q * C : (q + 1) * C, :] = turned[2 * C :]

    def tapped(grad):
        wide = grad.astype(F32)
        return jnp.concatenate(
            [pltpu.roll(wide, W - 1, 1).astype(BF), grad, pltpu.roll(wide, 1, 1).astype(BF)], axis=0
        )

    def pair_and_scatter(k):
        pltpu.make_async_copy(cr.at[k], cr.at[k], crr.at[k]).wait()
        for jx in range(2):
            for jy in range(3):
                j = 3 * jx + jy
                cs[k, j] = (dwf[k, core, j].astype(F32) + cr[k, j].astype(F32)).astype(BF)
                near = x_lo == jx
                far_x = lax.rem(x + (1 if jy % 2 == 0 else 3), 4)
                home = at(jnp.where(near, x, far_x), jy, z)
                slot = jnp.where(near, y, 4 + y)
                mine = jnp.logical_and(near, y == jy)

                @pl.when(mine)
                def _():
                    r2[k, slot] = cs[k, j]

                @pl.when(jnp.logical_not(mine))
                def _():
                    remote(cs.at[k, j], r2.at[k, slot], r2s.at[k, j], r2r.at[k, slot], home).start()

    def unit_lat(k, u):
        return lax.rem((nlat // 3) * u + 2 * k, nlat)

    def sum_and_scatter(k):
        @pl.when(y < 3)
        def _():
            total = r2[k, y].astype(F32)
            for d in range(1, 4):
                src = lax.rem(y + d, 4)
                pltpu.make_async_copy(r2.at[k, src], r2.at[k, src], r2r.at[k, src]).wait()
                total = total + r2[k, src].astype(F32)
            for src in range(4, 8):
                pltpu.make_async_copy(r2.at[k, src], r2.at[k, src], r2r.at[k, src]).wait()
                total = total + r2[k, src].astype(F32)
            st2[k] = total.astype(BF).reshape(UNITS, piece // UNITS, lanes)
            for u in range(UNITS):
                goal = unit_lat(k, u)

                @pl.when(goal != lat)
                def _():
                    dev = {"segment": seg, "lat": goal, "dp": core}
                    remote(st2.at[k, u], r3.at[k, lat], r3s.at[k, u], r3r.at[k, lat], dev).start()

    def lat_sum(k):
        for u in range(UNITS):
            @pl.when(jnp.logical_and(y < 3, unit_lat(k, u) == lat))
            def _():
                unit = st2[k, u].astype(F32)
                for d in range(1, nlat):
                    src = lax.rem(lat + d, nlat)
                    pltpu.make_async_copy(r3.at[k, src], r3.at[k, src], r3r.at[k, src]).wait()
                    unit = unit + r3[k, src].astype(F32)
                red[k, u] = unit.astype(BF)
                for d in range(1, nlat):
                    dev = {"segment": seg, "lat": lax.rem(lat + d, nlat), "dp": core}
                    remote(red.at[k, u], red.at[k, u], r4s.at[k, d], r4r.at[k, u], dev).start()

    my_piece = 3 * x_lo + jnp.minimum(y, 2)

    def deliver(k):
        @pl.when(y < 3)
        def _():
            for u in range(UNITS):
                @pl.when(unit_lat(k, u) != lat)
                def _():
                    pltpu.make_async_copy(red.at[k, u], red.at[k, u], r4r.at[k, u]).wait()

            @pl.when(seg == k)
            def _():
                gw_ref[core, my_piece] = red[k]

            @pl.when(seg != k)
            def _():
                dev = {"segment": k, "lat": lat, "dp": core}
                remote(red.at[k], gw_ref.at[core, my_piece], r5s.at[k], r5r.at[my_piece], dev).start()

    def staged(a, first=0):
        for lag, stage in ((1, pair_and_scatter), (4, sum_and_scatter), (6, lat_sum), (8, deliver))[first:]:
            k = a + lag

            @pl.when(jnp.logical_and(k >= 0, k < SECTIONS))
            def _():
                stage(k)

    def weight_work(k):
        later = k + SECTIONS
        taps = jnp.concatenate([tapped(gbuf[k + 1, 2]), tapped(gbuf[later + 1, 2])], axis=1)
        acts = jnp.concatenate([pbuf[k], pbuf[later]], axis=1)
        dw = lax.dot_general(taps, acts, (((1,), (1,)), ((), ())), preferred_element_type=F32)
        dwf[k] = dw.astype(BF).reshape(2, PIECES, piece, lanes)
        remote(dwf.at[k, other], cr.at[k], crs.at[k], crr.at[k], partner).start()

    def adjoint_out(k):
        @pl.when(k < SECTIONS)
        def _():
            out_send(gbuf.at[k, 2], sa_ref, 1, k)

    def backward(t, with_weights):
        b = 2 * t + 1
        a = 2 * t
        step = APPS - 1 - t
        halo_start(gbuf, b + 1, step)
        if with_weights:
            adjoint_out(b + 2)
            adjoint_out(b + 1)
        else:
            @pl.when(b == APPS - 1)
            def _():
                state_out(jnp.int32(APPS - 1))
                state_out(jnp.int32(APPS))
        turned_weights(lax.rem(b, SECTIONS), 0)
        turned_weights(lax.rem(a, SECTIONS), 1)
        if with_weights:
            @pl.when(b < SECTIONS - 1)
            def _():
                weight_work(b + 1)
                staged(b + 1)

            weight_work(b)
            staged(b)
        halo_wait(gbuf, b + 1, step)
        g = [gbuf[b + 1, i] for i in range(5)]
        sums = (
            jnp.dot(b2[0, 2], beside_each_other(g[1], g[2], g[3]), preferred_element_type=F32)
            + jnp.dot(b2[0, 0], beside_each_other(g[0], g[1], g[2]), preferred_element_type=F32)
            + jnp.dot(b2[0, 1], beside_each_other(g[2], g[3], g[4]), preferred_element_type=F32)
        )
        grads = []
        for m in range(3):
            moved = shifted_sum(sums[:, m * W : (m + 1) * W], 1)
            slope = silu_slope(sbuf[b, 1 + m].astype(F32))
            value = kept(m - 1, (g[1 + m].astype(F32) + slope * moved).astype(BF))
            gbuf[b, 1 + m] = value
            grads.append(value)
        sums = (
            jnp.dot(b2[1, 2], grads[1], preferred_element_type=F32)
            + jnp.dot(b2[1, 0], grads[0], preferred_element_type=F32)
            + jnp.dot(b2[1, 1], grads[2], preferred_element_type=F32)
        )
        slope = silu_slope(sbuf[a, 2].astype(F32))
        adjoint = grads[1].astype(F32) + slope * shifted_sum(sums, 1)
        if not with_weights:
            adjoint = adjoint + jnp.where(a == SECTIONS, xc[2].astype(F32), 0.0)
        gbuf[a, 2] = adjoint.astype(BF)

    def backward_late(i, carry):
        backward(APPS // 2 - 1 - i, False)
        return carry

    def backward_early(i, carry):
        backward(SECTIONS // 2 - 1 - i, True)
        return carry

    lax.fori_loop(0, (APPS - SECTIONS) // 2, backward_late, 0)
    lax.fori_loop(0, SECTIONS // 2, backward_early, 0)
    weight_work(jnp.int32(0))
    pair_and_scatter(jnp.int32(1))
    pair_and_scatter(jnp.int32(0))
    adjoint_out(jnp.int32(1))
    adjoint_out(jnp.int32(0))
    staged(jnp.int32(0), 1)

    def drain(i, carry):
        staged(-1 - i, 1)
        return carry

    lax.fori_loop(0, 8, drain, 0)
    for j in range(PIECES):
        @pl.when(seg != (j // 3) * 4 + j % 3)
        def _():
            pltpu.make_async_copy(gw_ref.at[core, j], gw_ref.at[core, j], r5r.at[j]).wait()
    last = remote(gw_ref.at[core], gw_ref.at[core], r6.at[0], r6.at[1], partner)
    last.start()

    for copy in sends:
        copy.wait_send()
    for j in range(4):
        beside_copy((1 - x_lo) * 4 + j).wait_send()
    for k in range(SECTIONS):
        for which, (dst, src) in enumerate(
            ((so_ref, sbuf.at[APPS - SECTIONS + k + 1, 2]), (sa_ref, gbuf.at[k, 2]))
        ):
            @pl.when(jnp.logical_not(is_self(k)))
            def _():
                out_copy(src, dst, which, k).wait_send()

    for what in range(2):
        for r in range(2):
            @pl.when(leaves(r))
            def _():
                given(r, what).wait_send()

    for s in range(8):
        from_self = jnp.logical_and(stays, jnp.logical_and(core == s % 2, y == s // 2))
        for which, dst in enumerate((so_ref, sa_ref)):
            @pl.when(jnp.logical_not(from_self))
            def _():
                pltpu.make_async_copy(dst.at[s], dst.at[s], ors.at[which, s]).wait()

    def ended(k, carry):
        pltpu.make_async_copy(dwf.at[k, other], dwf.at[k, other], crs.at[k]).wait()
        for j in range(PIECES):
            @pl.when(seg != (j // 3) * 4 + j % 3)
            def _():
                pltpu.make_async_copy(cs.at[k, j], cs.at[k, j], r2s.at[k, j]).wait()

        @pl.when(y < 3)
        def _():
            for u in range(UNITS):
                mine = unit_lat(k, u) == lat

                @pl.when(jnp.logical_not(mine))
                def _():
                    pltpu.make_async_copy(st2.at[k, u], st2.at[k, u], r3s.at[k, u]).wait()

                @pl.when(mine)
                def _():
                    for d in range(1, nlat):
                        pltpu.make_async_copy(red.at[k, u], red.at[k, u], r4s.at[k, d]).wait()

            @pl.when(seg != k)
            def _():
                pltpu.make_async_copy(red.at[k], red.at[k], r5s.at[k]).wait()

        return carry

    lax.fori_loop(0, SECTIONS, ended, 0)
    last.wait_send()
    pltpu.make_async_copy(gw_ref.at[other], gw_ref.at[other], r6.at[1]).wait()
    grads = gw_ref[...].reshape(K3, lanes).astype(F32) * normalizer
    for q in range(3):
        block = grads[q * C : (q + 1) * C]
        kg_ref[q] = block[:, 0:C]
        kg_ref[6 + q] = block[:, C : 2 * C]
        kg_ref[3 + q] = block[:, 2 * C : K3]
        if q == 1:
            bg_ref[...] = block[:, lanes - 128 :].T[K3 - lanes + 128 : K3 - lanes + 129]


def per_device(nz, initial, kernel, bias, cotangent):
    y = lax.rem(lax.axis_index("segment"), 4)
    C, W = initial.shape[1], initial.shape[3]
    K3 = 3 * C
    lanes = -(-(K3 + 2) // 128) * 128
    half, part = K3 // 2, K3 // 4
    nlat = 2 * nz
    piece = half // PIECES
    unit = piece // UNITS

    normalizer = 1.0 / math.sqrt(initial.shape[0] * 2 * initial.shape[2] * nlat * W)
    rows = jnp.stack([
        lax.dynamic_index_in_dim(band, y, 0, keepdims=False)
        for band in (initial, cotangent[1], cotangent[0])
    ]).transpose(2, 0, 1, 3)
    weights = kernel[0].transpose(1, 0, 2)
    offsets = jnp.broadcast_to(bias[0][:, None], (C, 128))

    vm = pl.BlockSpec(memory_space=pltpu.VMEM)
    dma = pltpu.SemaphoreType.DMA
    so, sa, kg, bg = pl.pallas_call(
        functools.partial(network_kernel, (C, W, nz), normalizer),
        out_shape=(
            jax.ShapeDtypeStruct((8, C, W), BF),
            jax.ShapeDtypeStruct((8, C, W), BF),
            jax.ShapeDtypeStruct((9, C, C), F32),
            jax.ShapeDtypeStruct((1, C), F32),
        ),
        in_specs=[vm, vm, vm],
        out_specs=(vm, vm, vm, vm),
        scratch_shapes=[
            pltpu.VMEM((2, PIECES, UNITS, unit, lanes), BF),
            pltpu.VMEM((3, C, W), BF),
            pltpu.VMEM((SECTIONS, 2, 2, part, lanes), BF),
            pltpu.VMEM((2, 3, K3, C), BF),
            pltpu.VMEM((APPS, lanes, W), BF),
            pltpu.VMEM((APPS + 1, 5, C, W), BF),
            pltpu.VMEM((APPS + 1, 5, C, W), BF),
            pltpu.VMEM((SECTIONS, 2, PIECES, piece, lanes), BF),
            pltpu.VMEM((SECTIONS, PIECES, piece, lanes), BF),
            pltpu.VMEM((SECTIONS, PIECES, piece, lanes), BF),
            pltpu.VMEM((SECTIONS, 8, piece, lanes), BF),
            pltpu.VMEM((SECTIONS, UNITS, unit, lanes), BF),
            pltpu.VMEM((SECTIONS, nlat, unit, lanes), BF),
            pltpu.VMEM((SECTIONS, UNITS, unit, lanes), BF),
            dma((2, 4)),
            dma((21,)),
            dma((22,)),
            dma((APPS, 5)),
            dma((APPS, 5)),
            dma((2, SECTIONS)),
            dma((2, 8)),
            dma((SECTIONS,)),
            dma((SECTIONS,)),
            dma((SECTIONS, PIECES)),
            dma((SECTIONS, 8)),
            dma((SECTIONS, UNITS)),
            dma((SECTIONS, nlat)),
            dma((SECTIONS, nlat)),
            dma((SECTIONS, UNITS)),
            dma((SECTIONS,)),
            dma((PIECES,)),
            dma((2,)),
        ],
        compiler_params=pltpu.CompilerParams(
            collective_id=0, has_side_effects=True, vmem_limit_bytes=60 * 2**20
        ),
    )(rows, weights, offsets)

    def banded(slots):
        return slots.reshape(4, 2, C, W).transpose(0, 2, 1, 3)[None]

    return (
        banded(so),
        banded(sa).astype(F32),
        kg.transpose(1, 0, 2)[None],
        bg,
    )


def solution(mesh):
    nz = mesh.shape["lat"] // 2
    return jax.shard_map(
        functools.partial(per_device, nz),
        mesh=mesh,
        in_specs=(
            P("dp", None, "lat", None),
            P("segment", None, None, None),
            P("segment", None),
            P(None, "dp", None, "lat", None),
        ),
        out_specs=(
            P("segment", "dp", None, "lat", None),
            P("segment", "dp", None, "lat", None),
            P("segment", None, None, None),
            P("segment", None),
        ),
        check_vma=False,
    )
```
